32 devices in a mesh: group: 2 (over y), ctx: 4 (over x, core), head: 4 (over z).
Axes of the slice: x: 2, y: 2, z: 4, core: 2. Of those that a mesh axis runs over, the one named last changes fastest.
Arguments:
- activations: bfloat16 [4096, 2304], P(('group', 'ctx', 'head')), parts along dimension 0, may hold values from -6 to 6
- w_query: bfloat16 [2304, 4096], P(None, 'head'), may hold values from -0.125 to 0.125
- w_key: bfloat16 [2304, 4096], P(None, 'head'), may hold values from -0.125 to 0.125
- w_value: bfloat16 [2304, 4096], P(None, 'head'), may hold values from -0.125 to 0.125
- conv_weight: float32 [4, 3, 4096], P(None, None, 'head'), may hold values from -3 to 3
- gate_down: bfloat16 [2304, 128], replicated, may hold values from -0.125 to 0.125
- gate_up: bfloat16 [128, 4096], P(None, 'head'), may hold values from -0.5 to 0.5
- w_beta: bfloat16 [2304, 32], P(None, 'head'), may hold values from -0.125 to 0.125
- decay_rate: float32 [32], P('head'), may hold values from 0 to 1, as said below
- fork_pos: int32 [4], P('group'), parts along dimension 0, may hold values from 0 to 2047, as said below
Outputs:
- attended: bfloat16 [4096, 4096], P(('group', 'ctx'), 'head'), parts along dimension 0
- fork_states: float32 [4, 32, 128, 128], P('group', 'head'), parts along dimension 0
The draws below stay inside these ranges and needn't reach their ends.
There are 2 independent parts, one for each index of `group`. The reference program is written for one: setup_inputs(seed, part) draws one part's arguments, and reference() takes and returns one part's arrays. A program takes and returns all parts, laid end to end along the dimension named above; an argument that names none is the same for every part. Nothing has to cross between parts.
Inputs may be any that keep to these rules, and one draw needn't show every extreme that they name: fork_pos[f] lies in [f * 1024, (f + 1) * 1024); the last one is 2047. `decay_rate`: positive rates.
All inputs are finite; a program needn't handle non-finite values.
Results may differ from the reference program's by a relative error of at most 0.0065.
Values may be sent and summed in bfloat16 or wider, within the bound.
A program may use at most 128 MiB of HBM per device.

```python
import math
import jax
import jax.numpy as jnp
from jax import lax

D = 2304
HEADS = 32
DK = 128
GATE_RANK = 128
CONV = 4
FORK = 1024
TOKENS = 2048
FORKS = 2


def draw_decay_rate(key, part):
    key_order, key_slow, key_fast = jax.random.split(jax.random.fold_in(key, 11), 3)
    order = jax.random.permutation(key_order, HEADS)
    slow_count = HEADS // 2
    slow_rates = jnp.exp(jax.random.uniform(key_slow, (HEADS,), jnp.float32, math.log(0.3 / TOKENS), math.log(2.0 / TOKENS)))
    fast_rates = jnp.exp(jax.random.uniform(key_fast, (HEADS,), jnp.float32, math.log(0.02), math.log(0.08)))
    return jnp.where(order < slow_count, slow_rates, fast_rates).astype(jnp.float32)


def draw_fork_pos(key, part):
    offsets = jax.random.randint(jax.random.fold_in(key, 23), (FORKS,), 0, FORK)
    index = jnp.arange(FORKS, dtype=jnp.int32)
    positions = index * FORK + offsets
    return jnp.where(index == FORKS - 1, TOKENS - 1, positions).astype(jnp.int32)


def steps_of(own_key, shape, pieces, least, largest):
    level, own = 1.0, jax.random.fold_in(own_key, 6)
    for axis_at, shards_of in pieces:
        steps = jnp.exp(jax.random.uniform(jax.random.fold_in(own, axis_at), (shards_of,), jnp.float32, least / len(pieces), largest / len(pieces)))
        level = level * jnp.repeat(steps, shape[axis_at] // shards_of).reshape([-1 if axis == axis_at else 1 for axis in range(len(shape))])
    return level


def bell_draw(stream_key, extent, width, most, shards=(), held_as=jnp.bfloat16):
    factor_of = steps_of(stream_key, extent, shards, -0.22, 0.18) if shards else 1.0
    drawn = jax.random.normal(stream_key, extent, jnp.float32) * width * factor_of
    return jnp.minimum(jnp.maximum(drawn, -most), most).astype(held_as)


def setup_inputs(seed: int = 0, part: int = 0) -> dict:
    key_list = jax.random.split(jax.random.key(seed), 11)
    part_splits = jax.random.split(jax.random.fold_in(key_list[10], part), 11)
    activations = bell_draw(part_splits[0], (TOKENS, D), 1.0, 6.0, ((0, 16),))
    w_query = bell_draw(key_list[1], (D, HEADS * DK), D ** -0.5, 0.125, ((1, 4),))
    w_key = bell_draw(key_list[2], (D, HEADS * DK), D ** -0.5, 0.125, ((1, 4),))
    w_value = bell_draw(key_list[3], (D, HEADS * DK), D ** -0.5, 0.125, ((1, 4),))
    conv_weight = bell_draw(key_list[4], (CONV, 3, HEADS * DK), CONV ** -0.5, 3.0, ((2, 4),), jnp.float32)
    gate_down = bell_draw(key_list[5], (D, GATE_RANK), D ** -0.5, 0.125)
    gate_up = bell_draw(key_list[6], (GATE_RANK, HEADS * DK), GATE_RANK ** -0.5, 0.5, ((1, 4),))
    w_beta = bell_draw(key_list[7], (D, HEADS), D ** -0.5, 0.125, ((1, 4),))
    decay_rate = draw_decay_rate(jax.random.fold_in(key_list[10], 71), part)
    fork_pos = draw_fork_pos(jax.random.fold_in(jax.random.fold_in(key_list[10], part), 71), part)
    return {"activations": activations, "w_query": w_query, "w_key": w_key, "w_value": w_value, "conv_weight": conv_weight, "gate_down": gate_down, "gate_up": gate_up, "w_beta": w_beta, "decay_rate": decay_rate, "fork_pos": fork_pos}


EXACT_MATMUL = lax.Precision.HIGHEST

def token_step(carried, inputs):
    memory_state, saved = carried
    query_vector, key, value, decay, strength, position, target = inputs
    faded_state = jnp.exp(decay)[:, :, None] * memory_state
    value_guess = jnp.einsum('oeg,oe->og', faded_state, key, precision=EXACT_MATMUL)
    update = strength[:, None] * (value - value_guess)
    memory_state = faded_state + key[:, :, None] * update[:, None, :]
    output_rows = jnp.einsum('oeg,oe->og', memory_state, query_vector, precision=EXACT_MATMUL)
    saved = jnp.where(position == target, memory_state, saved)
    return ((memory_state, saved), output_rows)

def fork_block(memory_state, inputs):
    query_vector, key, value, decay, strength, positions, target = inputs
    saved = jnp.zeros_like(memory_state)
    value_targets = jnp.broadcast_to(target, positions.shape)
    (memory_state, saved), outputs = lax.scan(token_step, (memory_state, saved), (query_vector, key, value, decay, strength, positions, value_targets))
    return (memory_state, (outputs, saved))

def reference(activations, w_query, w_key, w_value, conv_weight, gate_down, gate_up, w_beta, decay_rate, fork_pos):
    projected = jnp.stack([jnp.dot(activations, weights, preferred_element_type=jnp.float32).astype(jnp.bfloat16) for weights in (w_query, w_key, w_value)])
    taps = conv_weight.shape[0]
    head_cols = HEADS * DK
    extended = jnp.concatenate([jnp.zeros((3, taps - 1, head_cols), jnp.float32), projected.astype(jnp.float32)], axis=1)
    mixed = sum((conv_weight[tap][:, None, :] * extended[:, tap:tap + TOKENS, :] for tap in range(taps)))
    activated = jax.nn.silu(mixed).reshape(3, TOKENS, HEADS, DK)
    query_vector = activated[0] * lax.rsqrt(lax.optimization_barrier(jnp.sum(jnp.square(activated[0]), axis=-1, keepdims=True)) + 1e-06) / math.sqrt(DK)
    key = activated[1] * lax.rsqrt(lax.optimization_barrier(jnp.sum(jnp.square(activated[1]), axis=-1, keepdims=True)) + 1e-06)
    value = activated[2]
    latent = jnp.dot(activations, gate_down, preferred_element_type=jnp.float32).astype(jnp.bfloat16)
    gate_pre = jnp.dot(latent, gate_up, preferred_element_type=jnp.float32).reshape(TOKENS, HEADS, DK)
    log_decay = -decay_rate[None, :, None] * jax.nn.softplus(gate_pre)
    beta = jax.nn.sigmoid(jnp.dot(activations, w_beta, preferred_element_type=jnp.float32))
    positions = jnp.arange(TOKENS, dtype=jnp.int32).reshape(FORKS, FORK)

    def split_forks(values):
        return values.reshape((FORKS, FORK) + values.shape[1:])
    start_state = jnp.zeros((HEADS, DK, DK), jnp.float32)
    blocks_in = (split_forks(query_vector), split_forks(key), split_forks(value), split_forks(log_decay), split_forks(beta), positions, fork_pos.astype(jnp.int32))
    final_state, (outputs, saved) = lax.scan(fork_block, start_state, blocks_in)
    attended = outputs.reshape(TOKENS, HEADS * DK).astype(jnp.bfloat16)
    return (attended, saved)
```

```python
import functools
import math

import jax
import jax.numpy as jnp
from jax import lax
from jax.experimental import pallas as pl
from jax.experimental.pallas import tpu as pltpu
from jax.sharding import PartitionSpec as P

CHUNK = 128
F32 = jnp.float32
BF16 = jnp.bfloat16
NT = (((1,), (1,)), ((), ()))
TN = (((0,), (0,)), ((), ()))


def dot(left, right, dims=None):
    left, right = left.astype(BF16), right.astype(BF16)
    if dims is None:
        return jnp.dot(left, right, preferred_element_type=F32)
    return lax.dot_general(left, right, dims, preferred_element_type=F32)


def softplus(value):
    return jnp.maximum(value, 0.0) + jnp.log1p(jnp.exp(-jnp.abs(value)))


def level_masks():
    row = lax.broadcasted_iota(jnp.int32, (CHUNK, CHUNK), 0)
    col = lax.broadcasted_iota(jnp.int32, (CHUNK, CHUNK), 1)
    masks = {}
    size = 1
    while size < CHUNK:
        same = (row // (2 * size)) == (col // (2 * size))
        masks[size] = same & ((row & size) != 0) & ((col & size) == 0)
        size *= 2
    return row, col, masks


def level_reference(cum, size):
    if size >= 8:
        parts = cum.reshape(CHUNK // (2 * size), 2 * size, cum.shape[1])
        ref = parts[:, size - 1 : size, :]
        return jnp.broadcast_to(ref, parts.shape).reshape(cum.shape)
    parts = cum.reshape(CHUNK // 8, 8, cum.shape[1])
    place = lax.broadcasted_iota(jnp.int32, parts.shape, 1)
    ref = jnp.broadcast_to(parts[:, size - 1 : size, :], parts.shape)
    for start in range(2 * size, 8, 2 * size):
        ref = jnp.where(place >= start, parts[:, start + size - 1 : start + size, :], ref)
    return ref.reshape(cum.shape)


def local_kernel(
    q_ref, k_ref, v_ref, halo_ref, conv_ref, latent_ref, up_ref, beta_ref, rate_ref, pos_ref,
    w_ref, u_ref, qk_ref, qup_ref, kend_ref, dec_ref, kf_ref, df_ref, dev_ref, ext_ref,
):
    head = pl.program_id(0)
    seq_len, dim = q_ref.shape
    acts = []
    for j, src in enumerate((q_ref, k_ref, v_ref)):
        ext_ref[j, 0:8, :] = halo_ref[j].astype(F32)
        ext_ref[j, 8:, :] = src[...].astype(F32)
        taps = conv_ref.shape[0]
        mixed = sum(
            conv_ref[tap, j : j + 1, :] * ext_ref[j, 9 - taps + tap : 9 - taps + tap + seq_len, :]
            for tap in range(taps)
        )
        acts.append(mixed / (1.0 + jnp.exp(-mixed)))
    query = acts[0] * (
        lax.rsqrt(jnp.sum(acts[0] * acts[0], axis=-1, keepdims=True) + 1e-06) / math.sqrt(dim)
    )
    key = acts[1] * lax.rsqrt(jnp.sum(acts[1] * acts[1], axis=-1, keepdims=True) + 1e-06)
    value = acts[2]
    gate = jnp.dot(latent_ref[...], up_ref[...], preferred_element_type=F32)
    decay = -rate_ref[head] * softplus(gate)
    lane = lax.broadcasted_iota(jnp.int32, beta_ref.shape, 1)
    beta = jnp.sum(jnp.where(lane == head, beta_ref[...], 0.0), axis=1, keepdims=True)
    beta = 1.0 / (1.0 + jnp.exp(-beta))
    row, col, masks = level_masks()
    tril = (row >= col).astype(BF16)
    eye = (row == col).astype(F32)
    pos = pos_ref[0]
    stacked = jnp.concatenate([eye, jnp.zeros((dim, dim), F32)], axis=0)
    kf_ref[0] = jnp.zeros((CHUNK, dim), BF16)
    df_ref[0] = jnp.zeros((8, dim), F32)
    for c in range(seq_len // CHUNK):
        rows = slice(c * CHUNK, (c + 1) * CHUNK)
        g, qc, kc, vc, bc = decay[rows], query[rows], key[rows], value[rows], beta[rows]
        high = g.astype(BF16)
        low = (g - high.astype(F32)).astype(BF16)
        both = jnp.dot(tril, jnp.concatenate([high, low], axis=1), preferred_element_type=F32)
        cum = both[:, :dim] + both[:, dim:]
        pair_k = jnp.zeros((CHUNK, CHUNK), F32)
        pair_q = jnp.where(
            row == col, jnp.sum(qc.astype(BF16).astype(F32) * kc.astype(BF16).astype(F32), axis=1, keepdims=True), 0.0
        )
        for size, mask in masks.items():
            scale = jnp.exp(-jnp.abs(cum - level_reference(cum, size)))
            ks = (kc * scale).astype(BF16)
            qs = (qc * scale).astype(BF16)
            pairs = dot(jnp.concatenate([ks, qs], axis=0), ks, NT)
            pair_k = jnp.where(mask, pairs[:CHUNK], pair_k)
            pair_q = jnp.where(mask, pairs[CHUNK:], pair_q)
        system = bc * pair_k
        inverse = eye - jnp.where(masks[1], system, 0.0)
        for size, mask in masks.items():
            if size > 1:
                inverse = inverse - dot(dot(inverse, jnp.where(mask, system, 0.0)), inverse)
        grown = jnp.exp(cum)
        solved = dot(inverse, jnp.concatenate([bc * vc, bc * (kc * grown)], axis=1))
        u, w = solved[:, :dim], solved[:, dim:].astype(BF16)
        last = cum[CHUNK - 1 : CHUNK, :]
        kend = (kc * jnp.exp(last - cum)).astype(BF16)
        whole = jnp.exp(last)
        u_ref[rows, :] = u
        w_ref[rows, :] = w
        qk_ref[rows, :] = pair_q.astype(BF16)
        qup_ref[rows, :] = (qc * grown).astype(BF16)
        kend_ref[rows, :] = kend
        dec_ref[0, c : c + 1, :] = whole
        change = jnp.concatenate([jnp.zeros((CHUNK, dim), F32), u], axis=1) - dot(w, stacked, NT)
        stacked = stacked * whole + dot(change, kend, TN)

        @pl.when((pos >= c * CHUNK) & (pos < (c + 1) * CHUNK))
        def _():
            inner = pos - c * CHUNK
            at = jnp.sum(jnp.where(row[:, :1] == inner, cum, 0.0), axis=0, keepdims=True)
            keep = row[:, :1] <= inner
            kf_ref[0] = jnp.where(keep, kc * jnp.exp(jnp.minimum(at - cum, 0.0)), 0.0).astype(BF16)
            df_ref[0] = jnp.broadcast_to(jnp.exp(at), (8, dim))

    dev_ref[0] = stacked


def read_kernel(
    start_ref, w_ref, u_ref, qk_ref, qup_ref, kend_ref, dec_ref, kf_ref, df_ref, pos_ref,
    out_ref, fork_ref,
):
    seq_len, dim = w_ref.shape
    state = start_ref[0]
    pos = pos_ref[0]
    fork_ref[0] = jnp.zeros((dim, dim), BF16)
    for c in range(seq_len // CHUNK):
        rows = slice(c * CHUNK, (c + 1) * CHUNK)
        both = dot(jnp.concatenate([w_ref[rows, :], qup_ref[rows, :]], axis=0), state, NT)
        change = (u_ref[rows, :] - both[:CHUNK]).astype(BF16)
        out_ref[rows, :] = (both[CHUNK:] + dot(qk_ref[rows, :], change)).astype(BF16)

        @pl.when((pos >= c * CHUNK) & (pos < (c + 1) * CHUNK))
        def _():
            saved = state * df_ref[0, 0:1, :] + dot(change, kf_ref[0], TN)
            fork_ref[0] = saved.T.astype(BF16)

        state = state * dec_ref[0, c : c + 1, :] + dot(change, kend_ref[rows, :], TN)


def shifted(value, axis, by):
    size = lax.axis_size(axis)
    pairs = [(i, i + by) for i in range(size) if 0 <= i + by < size]
    return lax.ppermute(value, axis, pairs)


def per_device(
    activations, w_query, w_key, w_value, conv_weight, gate_down, gate_up, w_beta, decay_rate, fork_pos
):
    gathered = lax.all_gather(activations, "head", axis=0, tiled=True)
    seq_len = gathered.shape[0]
    num_heads = w_beta.shape[1]
    head_cols = w_query.shape[1]
    dim = head_cols // num_heads
    num_ctx = lax.axis_size("ctx")
    num_forks = fork_pos.shape[0]
    per_fork = num_ctx // num_forks
    projected = [
        jnp.dot(gathered, weights, preferred_element_type=F32).astype(BF16)
        for weights in (w_query, w_key, w_value)
    ]
    halo = shifted(jnp.stack([p[seq_len - 8 :] for p in projected]), "ctx", 1)
    latent = jnp.dot(gathered, gate_down, preferred_element_type=F32).astype(BF16)
    beta_pre = jnp.dot(gathered, w_beta, preferred_element_type=F32)
    ctx = lax.axis_index("ctx")
    pos = lax.dynamic_slice(fork_pos, (ctx // per_fork,), (1,)) - ctx * seq_len
    chunks = seq_len // CHUNK

    column = pl.BlockSpec((seq_len, dim), lambda h: (0, h))
    per_head = lambda *shape: pl.BlockSpec((1,) + shape, lambda h: (h,) + (0,) * len(shape))
    smem = pl.BlockSpec(memory_space=pltpu.SMEM)
    whole = lambda *shape: pl.BlockSpec(shape, lambda h: (0,) * len(shape))
    cols = lambda dtype: jax.ShapeDtypeStruct((seq_len, head_cols), dtype)
    heads = lambda dtype, *shape: jax.ShapeDtypeStruct((num_heads,) + shape, dtype)
    w, u, qk, qup, kend, dec, kf, df, dev = pl.pallas_call(
        local_kernel,
        grid=(num_heads,),
        in_specs=[
            column, column, column,
            pl.BlockSpec((3, 8, dim), lambda h: (0, 0, h)),
            pl.BlockSpec((conv_weight.shape[0], 3, dim), lambda h: (0, 0, h)),
            whole(seq_len, latent.shape[1]),
            pl.BlockSpec((latent.shape[1], dim), lambda h: (0, h)),
            whole(seq_len, num_heads), smem, smem,
        ],
        out_specs=[
            column, column, column, column, column,
            per_head(chunks, dim), per_head(CHUNK, dim), per_head(8, dim), per_head(2 * dim, dim),
        ],
        out_shape=[
            cols(BF16), cols(F32), cols(BF16), cols(BF16), cols(BF16),
            heads(F32, chunks, dim), heads(BF16, CHUNK, dim), heads(F32, 8, dim), heads(F32, 2 * dim, dim),
        ],
        scratch_shapes=[pltpu.VMEM((3, seq_len + 8, dim), F32)],
        name="local",
    )(*projected, halo, conv_weight, latent, gate_up, beta_pre, decay_rate, pos)

    trans, offset = dev[:, :dim], dev[:, dim:]
    start = jnp.zeros((num_heads, dim, dim), F32)
    for turn in range(num_ctx - 1):
        end = offset if turn == 0 else offset + jnp.einsum(
            "hij,hjk->hik", start, trans, precision=lax.Precision.HIGH
        )
        start = shifted(end.astype(BF16), "ctx", 1).astype(F32)

    attended, fork_local = pl.pallas_call(
        read_kernel,
        grid=(num_heads,),
        in_specs=[
            per_head(dim, dim), column, column, column, column, column,
            per_head(chunks, dim), per_head(CHUNK, dim), per_head(8, dim), smem,
        ],
        out_specs=[column, per_head(dim, dim)],
        out_shape=[cols(BF16), heads(BF16, dim, dim)],
        name="read",
    )(start, w, u, qk, qup, kend, dec, kf, df, pos)
    everyone = lax.all_gather(fork_local, "ctx", axis=0)
    fork_states = everyone.reshape((num_forks, per_fork) + fork_local.shape).astype(F32).sum(axis=1)
    return attended, fork_states


def solution(mesh):
    return jax.shard_map(
        per_device,
        mesh=mesh,
        in_specs=(
            P(("group", "ctx", "head"), None),
            P(None, "head"),
            P(None, "head"),
            P(None, "head"),
            P(None, None, "head"),
            P(),
            P(None, "head"),
            P(None, "head"),
            P("head"),
            P("group"),
        ),
        out_specs=(P(("group", "ctx"), "head"), P("group", "head", None, None)),
        check_vma=False,
    )
```

```python
import functools
import math

import jax
import jax.numpy as jnp
from jax import lax
from jax.experimental import pallas as pl
from jax.experimental.pallas import tpu as pltpu
from jax.sharding import PartitionSpec as P

HALO = 16
MESH = pl.DeviceIdType.MESH
F32 = jnp.float32
BF16 = jnp.bfloat16
NT = (((1,), (1,)), ((), ()))
TN = (((0,), (0,)), ((), ()))


def dot(left, right, dims=None):
    left, right = left.astype(BF16), right.astype(BF16)
    if dims is None:
        return jnp.dot(left, right, preferred_element_type=F32)
    return lax.dot_general(left, right, dims, preferred_element_type=F32)


def softplus(value):
    return jnp.maximum(value, 0.0) + jnp.log1p(jnp.exp(-jnp.abs(value)))


def level_masks(chunk):
    row = lax.broadcasted_iota(jnp.int32, (chunk, chunk), 0)
    col = lax.broadcasted_iota(jnp.int32, (chunk, chunk), 1)
    masks = {}
    size = 1
    while size < chunk:
        differ = row ^ col
        masks[size] = (row > col) & (differ >= size) & (differ < 2 * size)
        size *= 2
    return row, col, masks


def level_reference(cum, size):
    chunk = cum.shape[0]
    if size >= 8:
        parts = cum.reshape(chunk // (2 * size), 2 * size, cum.shape[1])
        ref = parts[:, size - 1 : size, :]
        return jnp.broadcast_to(ref, parts.shape).reshape(cum.shape)
    parts = cum.reshape(chunk // 8, 8, cum.shape[1])
    place = lax.broadcasted_iota(jnp.int32, parts.shape, 1)
    ref = jnp.broadcast_to(parts[:, size - 1 : size, :], parts.shape)
    for start in range(2 * size, 8, 2 * size):
        ref = jnp.where(place >= start, parts[:, start + size - 1 : start + size, :], ref)
    return ref.reshape(cum.shape)


def copies_done(copies):
    for copy in copies:
        copy.wait()


def local_kernel(
    num_ctx, num_blocks,
    act_ref, wq_hbm, wk_hbm, wv_hbm, conv_ref, down_hbm, gu_ref, wb_ref, rate_ref, pos_ref,
    w_ref, u_ref, qk_ref, qup_ref, kend_ref, dec_ref, kf_ref, df_ref, dev_ref,
    buf, weights, down_ref, ext_ref, latent_ref, beta_ref,
    load_sem, own_sem, halo_send, halo_recv, right_sem, left_sem, recv_sem,
):
    chunk, width = act_ref.shape
    num_heads = rate_ref.shape[0]
    dim = gu_ref.shape[1] // num_heads
    group = min(4, num_heads)
    span = group * dim
    taps = conv_ref.shape[0]
    ctx, place = lax.axis_index("ctx"), lax.axis_index("head")
    rank = ctx * num_blocks + place
    ranks = num_ctx * num_blocks
    after, before = (rank + 1) % ranks, (rank + ranks - 1) % ranks
    next_id = {"ctx": after // num_blocks, "head": after % num_blocks}
    prev_id = {"ctx": before // num_blocks, "head": before % num_blocks}

    loads = [
        pltpu.make_async_copy(src, weights.at[j], load_sem.at[j])
        for j, src in enumerate((wq_hbm, wk_hbm, wv_hbm))
    ] + [pltpu.make_async_copy(down_hbm, down_ref, load_sem.at[3])]
    own = pltpu.make_async_copy(act_ref, buf.at[place, pl.ds(HALO, chunk)], own_sem)
    own.start()
    for copy in loads:
        copy.start()
    barrier = pltpu.get_barrier_semaphore()
    for other in (next_id, prev_id):
        pl.semaphore_signal(barrier, inc=1, device_id=other, device_id_type=MESH)
    pl.semaphore_wait(barrier, 2)
    halo = pltpu.make_async_remote_copy(
        src_ref=act_ref.at[pl.ds(chunk - HALO, HALO)],
        dst_ref=buf.at[after % num_blocks, pl.ds(0, HALO)],
        send_sem=halo_send, recv_sem=halo_recv, device_id=next_id, device_id_type=MESH,
    )
    halo.start()
    kf_ref[...] = jnp.zeros(kf_ref.shape, kf_ref.dtype)
    df_ref[...] = jnp.zeros(df_ref.shape, df_ref.dtype)
    own.wait()
    halo.wait()

    def to_right(i):
        block = jnp.maximum(place - i, 0)
        return pltpu.make_async_remote_copy(
            src_ref=buf.at[block], dst_ref=buf.at[block],
            send_sem=right_sem.at[i], recv_sem=recv_sem.at[block],
            device_id=next_id, device_id_type=MESH,
        )

    def to_left(i):
        block = jnp.minimum(place + i, num_blocks - 1)
        return pltpu.make_async_remote_copy(
            src_ref=buf.at[block], dst_ref=buf.at[block],
            send_sem=left_sem.at[i], recv_sem=recv_sem.at[block],
            device_id=prev_id, device_id_type=MESH,
        )

    def goes_right(i):
        return (place - i >= 0) & (place < num_blocks - 1) & (i < num_blocks - 1)

    def goes_left(i):
        return (place + i < num_blocks) & (place > 0) & (i < num_blocks - 1)

    row, col, masks = level_masks(chunk)
    eye = (row == col).astype(F32)
    tril = (row >= col).astype(BF16)
    heads = range(group)
    cut = lambda value, h: value[:, h * dim : (h + 1) * dim]

    def step(i, carry):
        @pl.when((i > 0) & (place - i >= 0))
        def _():
            to_right(i).wait_recv()

        @pl.when((i > 0) & (place + i < num_blocks))
        def _():
            to_left(i).wait_recv()

        @pl.when(goes_right(i))
        def _():
            to_right(i).start()

        @pl.when(goes_left(i))
        def _():
            to_left(i).start()

        @pl.when(i == 0)
        def _():
            copies_done(loads)

        over = (place + i) // num_blocks
        block = (place + i) * (1 - over) + (num_blocks - 1 - i) * over
        first_row = pl.multiple_of(block * chunk, chunk)
        rows = pl.ds(first_row, chunk)
        own_rows = buf[block, HALO:, :]
        latent_ref[...] = jnp.dot(own_rows, down_ref[...], preferred_element_type=F32).astype(BF16)
        beta_ref[...] = jnp.dot(own_rows, wb_ref[...], preferred_element_type=F32)
        halo_keep = jnp.where(ctx * num_blocks + block == 0, 0.0, 1.0).astype(F32)
        inner = pos_ref[0] - block * chunk
        here = (inner >= 0) & (inner < chunk)

        def head_group(hg, carry):
            cols = pl.ds(pl.multiple_of(hg * span, span), span)
            acts = []
            for j in range(3):
                proj = jnp.dot(buf[block], weights[j, :, cols], preferred_element_type=F32)
                proj = proj.astype(BF16).astype(F32)
                ext_ref[j, 0:HALO, :] = proj[:HALO] * halo_keep
                ext_ref[j, HALO:, :] = proj[HALO:]
                start = HALO + 1 - taps
                mixed = sum(
                    conv_ref[tap, j : j + 1, cols] * ext_ref[j, start + tap : start + tap + chunk, :]
                    for tap in range(taps)
                )
                acts.append(mixed / (1.0 + jnp.exp(-mixed)))

            def normed(value, factor):
                parts = []
                for h in heads:
                    part = cut(value, h)
                    total = jnp.sum(part * part, axis=-1, keepdims=True)
                    parts.append(part * (lax.rsqrt(total + 1e-06) * factor))
                return jnp.concatenate(parts, axis=1)

            query, key, value = normed(acts[0], 1.0 / math.sqrt(dim)), normed(acts[1], 1.0), acts[2]
            gate = softplus(jnp.dot(latent_ref[...], gu_ref[:, cols], preferred_element_type=F32))
            g = jnp.concatenate([cut(gate, h) * -rate_ref[hg * group + h] for h in heads], axis=1)
            lane = lax.broadcasted_iota(jnp.int32, beta_ref.shape, 1)
            betas = []
            for h in heads:
                pre = jnp.sum(jnp.where(lane == hg * group + h, beta_ref[...], 0.0), axis=1, keepdims=True)
                betas.append(1.0 / (1.0 + jnp.exp(-pre)))
            high = g.astype(BF16)
            low = (g - high.astype(F32)).astype(BF16)
            both = jnp.dot(tril, jnp.concatenate([high, low], axis=1), preferred_element_type=F32)
            cum = both[:, :span] + both[:, span:]
            product = query.astype(BF16).astype(F32) * key.astype(BF16).astype(F32)
            pair_k = [jnp.zeros((chunk, chunk), F32) for h in heads]
            pair_q = [
                jnp.where(row == col, jnp.sum(cut(product, h), axis=1, keepdims=True), 0.0) for h in heads
            ]
            for size, mask in masks.items():
                scale = jnp.exp(-jnp.abs(cum - level_reference(cum, size)))
                ks = (key * scale).astype(BF16)
                qs = (query * scale).astype(BF16)
                pairs = [
                    dot(jnp.concatenate([cut(ks, h), cut(qs, h)], axis=0), cut(ks, h), NT) for h in heads
                ]
                pair_k = [jnp.where(mask, p[:chunk], old) for p, old in zip(pairs, pair_k)]
                pair_q = [jnp.where(mask, p[chunk:], old) for p, old in zip(pairs, pair_q)]
            system = [betas[h] * pair_k[h] for h in heads]
            inverse = [eye - jnp.where(masks[1], system[h], 0.0) for h in heads]
            for size, mask in masks.items():
                if size > 1:
                    left = [dot(inverse[h], jnp.where(mask, system[h], 0.0)) for h in heads]
                    right = [dot(left[h], inverse[h]) for h in heads]
                    inverse = [inverse[h] - right[h] for h in heads]
            grown = jnp.exp(cum)
            key_up = key * grown
            last = cum[chunk - 1 : chunk, :]
            solved = [
                dot(inverse[h], jnp.concatenate([betas[h] * cut(value, h), betas[h] * cut(key_up, h)], axis=1))
                for h in heads
            ]
            u_ref[rows, cols] = jnp.concatenate([s[:, :dim] for s in solved], axis=1)
            w_ref[rows, cols] = jnp.concatenate([s[:, dim:] for s in solved], axis=1).astype(BF16)
            for h in heads:
                qk_ref[hg * group + h, rows, :] = pair_q[h].astype(BF16)
            qup_ref[rows, cols] = (query * grown).astype(BF16)
            kend_ref[rows, cols] = (key * jnp.exp(last - cum)).astype(BF16)
            whole = jnp.exp(last)
            at = jnp.sum(jnp.where(row[:, :1] == inner, cum, 0.0), axis=0, keepdims=True)
            keep = (row[:, :1] <= inner) & here
            kf_new = jnp.where(keep, key * jnp.exp(jnp.minimum(at - cum, 0.0)), 0.0)
            df_new = jnp.where(here, jnp.exp(at), 0.0)
            for h in heads:
                dec_ref[hg * group + h, pl.ds(block, 1), :] = cut(whole, h)
                kf_ref[hg * group + h] += cut(kf_new, h).astype(BF16)
                df_ref[hg * group + h] += jnp.broadcast_to(cut(df_new, h), (8, dim))
            return carry

        return lax.fori_loop(0, num_heads // group, head_group, carry)

    lax.fori_loop(0, num_blocks, step, 0)

    def compose(hg, carry):
        stacked = [jnp.concatenate([jnp.eye(dim, dtype=F32), jnp.zeros((dim, dim), F32)], axis=0) for h in heads]
        for c in range(num_blocks):
            rows = slice(c * chunk, (c + 1) * chunk)
            head_cols = [pl.ds(pl.multiple_of((hg * group + h) * dim, dim), dim) for h in heads]
            change = [
                jnp.concatenate([jnp.zeros((chunk, dim), F32), u_ref[rows, head_cols[h]]], axis=1)
                - dot(w_ref[rows, head_cols[h]], stacked[h], NT)
                for h in heads
            ]
            stacked = [
                stacked[h] * dec_ref[hg * group + h, c : c + 1, :]
                + dot(change[h], kend_ref[rows, head_cols[h]], TN)
                for h in heads
            ]
        for h in heads:
            dev_ref[hg * group + h] = stacked[h]
        return carry

    lax.fori_loop(0, num_heads // group, compose, 0)

    def drain(i, carry):
        @pl.when(goes_right(i))
        def _():
            to_right(i).wait_send()

        @pl.when(goes_left(i))
        def _():
            to_left(i).wait_send()

        return carry

    lax.fori_loop(0, num_blocks - 1, drain, 0)


def read_kernel(
    start_ref, w_ref, u_ref, qk_ref, qup_ref, kend_ref, dec_ref, kf_ref, df_ref, pos_ref,
    out_ref, fork_ref,
):
    seq_len, dim = w_ref.shape
    chunk = seq_len // dec_ref.shape[1]
    state = start_ref[0]
    pos = pos_ref[0]
    fork_ref[0] = jnp.zeros((dim, dim), BF16)
    for c in range(seq_len // chunk):
        rows = slice(c * chunk, (c + 1) * chunk)
        both = dot(jnp.concatenate([w_ref[rows, :], qup_ref[rows, :]], axis=0), state, NT)
        change = (u_ref[rows, :] - both[:chunk]).astype(BF16)
        out_ref[rows, :] = (both[chunk:] + dot(qk_ref[0, rows, :], change)).astype(BF16)

        @pl.when((pos >= c * chunk) & (pos < (c + 1) * chunk))
        def _():
            saved = state * df_ref[0, 0:1, :] + dot(change, kf_ref[0], TN)
            fork_ref[0] = saved.T.astype(BF16)

        state = state * dec_ref[0, c : c + 1, :] + dot(change, kend_ref[rows, :], TN)


def shifted(value, axis, by):
    size = lax.axis_size(axis)
    pairs = [(i, i + by) for i in range(size) if 0 <= i + by < size]
    return lax.ppermute(value, axis, pairs)


def per_device(
    activations, w_query, w_key, w_value, conv_weight, gate_down, gate_up, w_beta, decay_rate, fork_pos
):
    chunk, width = activations.shape
    num_blocks = lax.axis_size("head")
    seq_len = chunk * num_blocks
    num_heads = w_beta.shape[1]
    head_cols = w_query.shape[1]
    dim = head_cols // num_heads
    num_ctx = lax.axis_size("ctx")
    num_forks = fork_pos.shape[0]
    per_fork = num_ctx // num_forks
    ctx = lax.axis_index("ctx")
    pos = lax.dynamic_slice(fork_pos, (ctx // per_fork,), (1,)) - ctx * seq_len
    span = min(4, num_heads) * dim

    column = pl.BlockSpec((seq_len, dim), lambda h: (0, h))
    per_head = lambda *shape: pl.BlockSpec((1,) + shape, lambda h: (h,) + (0,) * len(shape))
    smem = pl.BlockSpec(memory_space=pltpu.SMEM)
    vmem = pl.BlockSpec(memory_space=pltpu.VMEM)
    hbm = pl.BlockSpec(memory_space=pl.ANY)
    cols = lambda dtype: jax.ShapeDtypeStruct((seq_len, head_cols), dtype)
    heads = lambda dtype, *shape: jax.ShapeDtypeStruct((num_heads,) + shape, dtype)
    w, u, qk, qup, kend, dec, kf, df, dev = pl.pallas_call(
        functools.partial(local_kernel, num_ctx, num_blocks),
        in_specs=[vmem, hbm, hbm, hbm, vmem, hbm, vmem, vmem, smem, smem],
        out_specs=[vmem] * 9,
        out_shape=[
            cols(BF16), cols(F32), heads(BF16, seq_len, chunk), cols(BF16), cols(BF16),
            heads(F32, num_blocks, dim), heads(BF16, chunk, dim), heads(F32, 8, dim), heads(F32, 2 * dim, dim),
        ],
        scratch_shapes=[
            pltpu.VMEM((num_blocks, HALO + chunk, width), BF16),
            pltpu.VMEM((3, width, head_cols), BF16),
            pltpu.VMEM((width, gate_down.shape[1]), BF16),
            pltpu.VMEM((3, HALO + chunk, span), F32),
            pltpu.VMEM((chunk, gate_down.shape[1]), BF16),
            pltpu.VMEM((chunk, num_heads), F32),
            pltpu.SemaphoreType.DMA((4,)),
            pltpu.SemaphoreType.DMA,
            pltpu.SemaphoreType.DMA,
            pltpu.SemaphoreType.DMA,
            pltpu.SemaphoreType.DMA((num_blocks,)),
            pltpu.SemaphoreType.DMA((num_blocks,)),
            pltpu.SemaphoreType.DMA((num_blocks,)),
        ],
        compiler_params=pltpu.CompilerParams(
            collective_id=0, has_side_effects=True, vmem_limit_bytes=60 << 20
        ),
        name="local",
    )(activations, w_query, w_key, w_value, conv_weight, gate_down, gate_up, w_beta, decay_rate, pos)

    trans, offset = dev[:, :dim], dev[:, dim:]
    start = jnp.zeros((num_heads, dim, dim), F32)
    for turn in range(num_ctx - 1):
        end = offset if turn == 0 else offset + jnp.einsum(
            "hij,hjk->hik", start, trans, precision=lax.Precision.HIGH
        )
        start = shifted(end.astype(BF16), "ctx", 1).astype(F32)

    attended, fork_local = pl.pallas_call(
        read_kernel,
        grid=(num_heads,),
        in_specs=[
            per_head(dim, dim), column, column, per_head(seq_len, chunk), column, column,
            per_head(num_blocks, dim), per_head(chunk, dim), per_head(8, dim), smem,
        ],
        out_specs=[column, per_head(dim, dim)],
        out_shape=[cols(BF16), heads(BF16, dim, dim)],
        name="read",
    )(start, w, u, qk, qup, kend, dec, kf, df, pos)
    everyone = lax.all_gather(fork_local, "ctx", axis=0)
    fork_states = everyone.reshape((num_forks, per_fork) + fork_local.shape).astype(F32).sum(axis=1)
    return attended, fork_states


def solution(mesh):
    return jax.shard_map(
        per_device,
        mesh=mesh,
        in_specs=(
            P(("group", "ctx", "head"), None),
            P(None, "head"),
            P(None, "head"),
            P(None, "head"),
            P(None, None, "head"),
            P(),
            P(None, "head"),
            P(None, "head"),
            P("head"),
            P("group"),
        ),
        out_specs=(P(("group", "ctx"), "head"), P("group", "head", None, None)),
        check_vma=False,
    )
```

```python
import functools
import math

import jax
import jax.numpy as jnp
from jax import lax
from jax.experimental import pallas as pl
from jax.experimental.pallas import tpu as pltpu
from jax.sharding import PartitionSpec as P

HALO = 16
MESH = pl.DeviceIdType.MESH
F32 = jnp.float32
BF16 = jnp.bfloat16
NT = (((1,), (1,)), ((), ()))
TN = (((0,), (0,)), ((), ()))


def dot(left, right, dims=None):
    left, right = left.astype(BF16), right.astype(BF16)
    if dims is None:
        return jnp.dot(left, right, preferred_element_type=F32)
    return lax.dot_general(left, right, dims, preferred_element_type=F32)


def softplus(value):
    return jnp.maximum(value, 0.0) + jnp.log1p(jnp.exp(-jnp.abs(value)))


def level_masks(chunk):
    row = lax.broadcasted_iota(jnp.int32, (chunk, chunk), 0)
    col = lax.broadcasted_iota(jnp.int32, (chunk, chunk), 1)
    masks = {}
    size = 1
    while size < chunk:
        differ = row ^ col
        masks[size] = (row > col) & (differ >= size) & (differ < 2 * size)
        size *= 2
    return row, col, masks


def level_reference(cum, size):
    chunk = cum.shape[0]
    if size >= 8:
        parts = cum.reshape(chunk // (2 * size), 2 * size, cum.shape[1])
        ref = parts[:, size - 1 : size, :]
        return jnp.broadcast_to(ref, parts.shape).reshape(cum.shape)
    parts = cum.reshape(chunk // 8, 8, cum.shape[1])
    place = lax.broadcasted_iota(jnp.int32, parts.shape, 1)
    ref = jnp.broadcast_to(parts[:, size - 1 : size, :], parts.shape)
    for start in range(2 * size, 8, 2 * size):
        ref = jnp.where(place >= start, parts[:, start + size - 1 : start + size, :], ref)
    return ref.reshape(cum.shape)


def copies_done(copies):
    for copy in copies:
        copy.wait()


def local_kernel(
    num_ctx, num_blocks,
    act_ref, wq_hbm, wk_hbm, wv_hbm, conv_ref, down_hbm, gu_ref, wb_ref, rate_ref, pos_ref,
    out_ref, forks_ref,
    w_ref, u_ref, qk_ref, qup_ref, kend_ref, dec_ref, kf_ref, df_ref,
    prefix_ref, change_ref, dev_ref, gain_ref, base_ref, fork_gain, fork_base,
    start_ref, end_ref, part_ref, other_ref, fork_ref,
    buf, weights, down_ref, ext_ref, latent_ref, beta_ref,
    load_sem, own_sem, halo_send, halo_recv, right_sem, left_sem, recv_sem,
    chain_send, chain_recv, pair_send, pair_recv, fork_send, fork_recv,
):
    chunk, width = act_ref.shape
    num_heads = rate_ref.shape[0]
    dim = gu_ref.shape[1] // num_heads
    group = min(4, num_heads)
    span = group * dim
    taps = conv_ref.shape[0]
    ctx, place = lax.axis_index("ctx"), lax.axis_index("head")
    rank = ctx * num_blocks + place
    ranks = num_ctx * num_blocks
    after, before = (rank + 1) % ranks, (rank + ranks - 1) % ranks
    next_id = {"ctx": after // num_blocks, "head": after % num_blocks}
    prev_id = {"ctx": before // num_blocks, "head": before % num_blocks}

    loads = [
        pltpu.make_async_copy(src, weights.at[j], load_sem.at[j])
        for j, src in enumerate((wq_hbm, wk_hbm, wv_hbm))
    ] + [pltpu.make_async_copy(down_hbm, down_ref, load_sem.at[3])]
    own = pltpu.make_async_copy(act_ref, buf.at[place, pl.ds(HALO, chunk)], own_sem)
    own.start()
    for copy in loads:
        copy.start()
    barrier = pltpu.get_barrier_semaphore()
    for other in (next_id, prev_id):
        pl.semaphore_signal(barrier, inc=1, device_id=other, device_id_type=MESH)
    for turn in range(1, num_ctx):
        pl.semaphore_signal(
            barrier, inc=1, device_id={"ctx": (ctx + turn) % num_ctx}, device_id_type=MESH
        )
    pl.semaphore_wait(barrier, num_ctx + 1)
    halo = pltpu.make_async_remote_copy(
        src_ref=act_ref.at[pl.ds(chunk - HALO, HALO)],
        dst_ref=buf.at[after % num_blocks, pl.ds(0, HALO)],
        send_sem=halo_send, recv_sem=halo_recv, device_id=next_id, device_id_type=MESH,
    )
    halo.start()
    kf_ref[...] = jnp.zeros(kf_ref.shape, kf_ref.dtype)
    df_ref[...] = jnp.zeros(df_ref.shape, df_ref.dtype)
    own.wait()
    halo.wait()

    def to_right(i):
        block = jnp.maximum(place - i, 0)
        return pltpu.make_async_remote_copy(
            src_ref=buf.at[block], dst_ref=buf.at[block],
            send_sem=right_sem.at[i], recv_sem=recv_sem.at[block],
            device_id=next_id, device_id_type=MESH,
        )

    def to_left(i):
        block = jnp.minimum(place + i, num_blocks - 1)
        return pltpu.make_async_remote_copy(
            src_ref=buf.at[block], dst_ref=buf.at[block],
            send_sem=left_sem.at[i], recv_sem=recv_sem.at[block],
            device_id=prev_id, device_id_type=MESH,
        )

    def goes_right(i):
        return (place - i >= 0) & (place < num_blocks - 1) & (i < num_blocks - 1)

    def goes_left(i):
        return (place + i < num_blocks) & (place > 0) & (i < num_blocks - 1)

    row, col, masks = level_masks(chunk)
    eye = (row == col).astype(F32)
    tril = (row >= col).astype(BF16)
    heads = range(group)
    cut = lambda value, h: value[:, h * dim : (h + 1) * dim]

    def step(i, carry):
        @pl.when((i > 0) & (place - i >= 0))
        def _():
            to_right(i).wait_recv()

        @pl.when((i > 0) & (place + i < num_blocks))
        def _():
            to_left(i).wait_recv()

        @pl.when(goes_right(i))
        def _():
            to_right(i).start()

        @pl.when(goes_left(i))
        def _():
            to_left(i).start()

        @pl.when(i == 0)
        def _():
            copies_done(loads)

        over = (place + i) // num_blocks
        block = (place + i) * (1 - over) + (num_blocks - 1 - i) * over
        first_row = pl.multiple_of(block * chunk, chunk)
        rows = pl.ds(first_row, chunk)
        own_rows = buf[block, HALO:, :]
        latent_ref[...] = jnp.dot(own_rows, down_ref[...], preferred_element_type=F32).astype(BF16)
        beta_ref[...] = jnp.dot(own_rows, wb_ref[...], preferred_element_type=F32)
        halo_keep = jnp.where(ctx * num_blocks + block == 0, 0.0, 1.0).astype(F32)
        inner = pos_ref[0] - block * chunk
        here = (inner >= 0) & (inner < chunk)

        def head_group(hg, carry):
            cols = pl.ds(pl.multiple_of(hg * span, span), span)
            acts = []
            for j in range(3):
                proj = jnp.dot(buf[block], weights[j, :, cols], preferred_element_type=F32)
                proj = proj.astype(BF16).astype(F32)
                ext_ref[j, 0:HALO, :] = proj[:HALO] * halo_keep
                ext_ref[j, HALO:, :] = proj[HALO:]
                start = HALO + 1 - taps
                mixed = sum(
                    conv_ref[tap, j : j + 1, cols] * ext_ref[j, start + tap : start + tap + chunk, :]
                    for tap in range(taps)
                )
                acts.append(mixed / (1.0 + jnp.exp(-mixed)))

            def normed(value, factor):
                parts = []
                for h in heads:
                    part = cut(value, h)
                    total = jnp.sum(part * part, axis=-1, keepdims=True)
                    parts.append(part * (lax.rsqrt(total + 1e-06) * factor))
                return jnp.concatenate(parts, axis=1)

            query, key, value = normed(acts[0], 1.0 / math.sqrt(dim)), normed(acts[1], 1.0), acts[2]
            gate = softplus(jnp.dot(latent_ref[...], gu_ref[:, cols], preferred_element_type=F32))
            g = jnp.concatenate([cut(gate, h) * -rate_ref[hg * group + h] for h in heads], axis=1)
            lane = lax.broadcasted_iota(jnp.int32, beta_ref.shape, 1)
            betas = []
            for h in heads:
                pre = jnp.sum(jnp.where(lane == hg * group + h, beta_ref[...], 0.0), axis=1, keepdims=True)
                betas.append(1.0 / (1.0 + jnp.exp(-pre)))
            high = g.astype(BF16)
            low = (g - high.astype(F32)).astype(BF16)
            both = jnp.dot(tril, jnp.concatenate([high, low], axis=1), preferred_element_type=F32)
            cum = both[:, :span] + both[:, span:]
            product = query.astype(BF16).astype(F32) * key.astype(BF16).astype(F32)
            pair_k = [jnp.zeros((chunk, chunk), F32) for h in heads]
            pair_q = [
                jnp.where(row == col, jnp.sum(cut(product, h), axis=1, keepdims=True), 0.0) for h in heads
            ]
            for size, mask in masks.items():
                scale = jnp.exp(-jnp.abs(cum - level_reference(cum, size)))
                ks = (key * scale).astype(BF16)
                qs = (query * scale).astype(BF16)
                pairs = [
                    dot(jnp.concatenate([cut(ks, h), cut(qs, h)], axis=0), cut(ks, h), NT) for h in heads
                ]
                pair_k = [jnp.where(mask, p[:chunk], old) for p, old in zip(pairs, pair_k)]
                pair_q = [jnp.where(mask, p[chunk:], old) for p, old in zip(pairs, pair_q)]
            system = [betas[h] * pair_k[h] for h in heads]
            inverse = [eye - jnp.where(masks[1], system[h], 0.0) for h in heads]
            for size, mask in masks.items():
                if size > 1:
                    left = [dot(inverse[h], jnp.where(mask, system[h], 0.0)) for h in heads]
                    right = [dot(left[h], inverse[h]) for h in heads]
                    inverse = [inverse[h] - right[h] for h in heads]
            grown = jnp.exp(cum)
            key_up = key * grown
            last = cum[chunk - 1 : chunk, :]
            solved = [
                dot(inverse[h], jnp.concatenate([betas[h] * cut(value, h), betas[h] * cut(key_up, h)], axis=1))
                for h in heads
            ]
            u_ref[rows, cols] = jnp.concatenate([s[:, :dim] for s in solved], axis=1)
            w_ref[rows, cols] = jnp.concatenate([s[:, dim:] for s in solved], axis=1).astype(BF16)
            for h in heads:
                qk_ref[hg * group + h, rows, :] = pair_q[h].astype(BF16)
            qup_ref[rows, cols] = (query * grown).astype(BF16)
            kend_ref[rows, cols] = (key * jnp.exp(last - cum)).astype(BF16)
            whole = jnp.exp(last)
            at = jnp.sum(jnp.where(row[:, :1] == inner, cum, 0.0), axis=0, keepdims=True)
            keep = (row[:, :1] <= inner) & here
            kf_new = jnp.where(keep, key * jnp.exp(jnp.minimum(at - cum, 0.0)), 0.0)
            df_new = jnp.where(here, jnp.exp(at), 0.0)
            for h in heads:
                dec_ref[hg * group + h, pl.ds(block, 1), :] = cut(whole, h)
                kf_ref[hg * group + h] += cut(kf_new, h).astype(BF16)
                df_ref[hg * group + h] += jnp.broadcast_to(cut(df_new, h), (8, dim))
            return carry

        return lax.fori_loop(0, num_heads // group, head_group, carry)

    lax.fori_loop(0, num_blocks, step, 0)

    def compose(hg, carry):
        stacked = [jnp.concatenate([jnp.eye(dim, dtype=F32), jnp.zeros((dim, dim), F32)], axis=0) for h in heads]
        for c in range(num_blocks):
            rows = slice(c * chunk, (c + 1) * chunk)
            head_cols = [pl.ds(pl.multiple_of((hg * group + h) * dim, dim), dim) for h in heads]
            change = [
                (
                    jnp.concatenate([jnp.zeros((chunk, dim), F32), u_ref[rows, head_cols[h]]], axis=1)
                    - dot(w_ref[rows, head_cols[h]], stacked[h], NT)
                ).astype(BF16)
                for h in heads
            ]
            for h in heads:
                prefix_ref[hg * group + h, c] = stacked[h]
                change_ref[hg * group + h, c] = change[h]
            stacked = [
                stacked[h] * dec_ref[hg * group + h, c : c + 1, :]
                + dot(change[h], kend_ref[rows, head_cols[h]], TN)
                for h in heads
            ]
        for h in heads:
            dev_ref[hg * group + h] = stacked[h]
        return carry

    groups = num_heads // group
    lax.fori_loop(0, groups, compose, 0)

    @pl.when(ctx == 0)
    def _():
        start_ref[...] = jnp.zeros(start_ref.shape, BF16)

    def pass_on(gi):
        part = pl.ds(gi * group, group)
        return pltpu.make_async_remote_copy(
            src_ref=end_ref.at[part], dst_ref=start_ref.at[part],
            send_sem=chain_send.at[gi], recv_sem=chain_recv.at[gi],
            device_id={"ctx": jnp.minimum(ctx + 1, num_ctx - 1)}, device_id_type=MESH,
        )

    def chain():
        def one(gi, carry):
            @pl.when(ctx > 0)
            def _():
                pass_on(gi).wait_recv()

            @pl.when(ctx < num_ctx - 1)
            def _():
                ends = []
                for h in heads:
                    trans = dev_ref[gi * group + h, :dim, :]
                    fine = (trans - trans.astype(BF16).astype(F32)).astype(BF16)
                    first = start_ref[gi * group + h]
                    ends.append(dot(first, trans) + dot(first, fine) + dev_ref[gi * group + h, dim:, :])
                for h in heads:
                    end_ref[gi * group + h] = ends[h].astype(BF16)
                pass_on(gi).start()

            return carry

        lax.fori_loop(0, groups, one, 0)

    pair = 2
    which = pos_ref[1]
    owned = (pos_ref[0] >= 0) & (pos_ref[0] < num_blocks * chunk)

    def read(j, carry):
        @pl.when(ctx == j)
        def _():
            chain()

        for p in range(pair):
            h = j * pair + p
            cols = pl.ds(pl.multiple_of(h * dim, dim), dim)
            for c in range(num_blocks):
                rows = slice(c * chunk, (c + 1) * chunk)
                both = dot(qup_ref[rows, cols], prefix_ref[h, c], NT) + dot(qk_ref[h, rows, :], change_ref[h, c])
                gain_ref[rows, cols] = both[:, :dim].astype(BF16)
                base_ref[rows, cols] = both[:, dim:]
            saved = prefix_ref[h, which] * df_ref[h, 0:1, :] + dot(change_ref[h, which], kf_ref[h], TN)
            fork_gain[h] = saved[:dim].T.astype(BF16)
            fork_base[h] = saved[dim:].T
        return carry

    parts = num_heads // pair
    lax.fori_loop(0, parts, read, 0)

    @pl.when(ctx >= parts)
    def _():
        chain()

    half = num_heads // 2
    core = ctx % 2
    mine = ctx // 2

    for h in range(num_heads):
        state = fork_base[h] + dot(fork_gain[h], start_ref[h], NT)
        part_ref[h] = jnp.where(owned, state, 0.0).astype(BF16)
    swap = pltpu.make_async_remote_copy(
        src_ref=part_ref.at[pl.ds((1 - core) * half, half)], dst_ref=other_ref,
        send_sem=pair_send, recv_sem=pair_recv,
        device_id={"ctx": mine * 2 + 1 - core}, device_id_type=MESH,
    )
    swap.start()

    def finish(h, carry):
        cols = pl.ds(pl.multiple_of(h * dim, dim), dim)
        out_ref[:, cols] = (base_ref[:, cols] + dot(gain_ref[:, cols], start_ref[h], NT)).astype(BF16)
        return carry

    lax.fori_loop(0, half, finish, 0)
    swap.wait()
    own_half = pl.ds(core * half, half)
    fork_ref[mine, own_half] = (part_ref[own_half].astype(F32) + other_ref[...].astype(F32)).astype(BF16)

    def share(turn, source):
        block = fork_ref.at[source // 2, pl.ds((source % 2) * half, half)]
        return pltpu.make_async_remote_copy(
            src_ref=block, dst_ref=block,
            send_sem=fork_send.at[turn], recv_sem=fork_recv.at[source],
            device_id={"ctx": (ctx + turn) % num_ctx}, device_id_type=MESH,
        )

    for turn in range(1, num_ctx):
        share(turn, ctx).start()
    lax.fori_loop(half, num_heads, finish, 0)
    for turn in range(1, num_ctx):
        share(turn, (ctx + turn) % num_ctx).wait_recv()
    for turn in range(1, num_ctx):
        share(turn, ctx).wait_send()
    forks_ref[...] = fork_ref[...].astype(F32)

    @pl.when(ctx < num_ctx - 1)
    def _():
        lax.fori_loop(0, groups, lambda gi, carry: (pass_on(gi).wait_send(), carry)[1], 0)

    def drain(i, carry):
        @pl.when(goes_right(i))
        def _():
            to_right(i).wait_send()

        @pl.when(goes_left(i))
        def _():
            to_left(i).wait_send()

        return carry

    lax.fori_loop(0, num_blocks - 1, drain, 0)


def per_device(
    activations, w_query, w_key, w_value, conv_weight, gate_down, gate_up, w_beta, decay_rate, fork_pos
):
    chunk, width = activations.shape
    num_blocks = lax.axis_size("head")
    seq_len = chunk * num_blocks
    num_heads = w_beta.shape[1]
    head_cols = w_query.shape[1]
    dim = head_cols // num_heads
    num_ctx = lax.axis_size("ctx")
    num_forks = fork_pos.shape[0]
    per_fork = num_ctx // num_forks
    ctx = lax.axis_index("ctx")
    assert per_fork == 2 and num_heads % 2 == 0
    pos = lax.dynamic_slice(fork_pos, (ctx // per_fork,), (1,)) - ctx * seq_len
    pos = jnp.concatenate([pos, jnp.clip(pos, 0, seq_len - 1) // chunk])
    span = min(4, num_heads) * dim

    smem = pl.BlockSpec(memory_space=pltpu.SMEM)
    vmem = pl.BlockSpec(memory_space=pltpu.VMEM)
    hbm = pl.BlockSpec(memory_space=pl.ANY)
    cols = lambda dtype: pltpu.VMEM((seq_len, head_cols), dtype)
    heads = lambda dtype, *shape: pltpu.VMEM((num_heads,) + shape, dtype)
    return pl.pallas_call(
        functools.partial(local_kernel, num_ctx, num_blocks),
        in_specs=[vmem, hbm, hbm, hbm, vmem, hbm, vmem, vmem, smem, smem],
        out_specs=[vmem] * 2,
        out_shape=[
            jax.ShapeDtypeStruct((seq_len, head_cols), BF16),
            jax.ShapeDtypeStruct((num_forks, num_heads, dim, dim), F32),
        ],
        scratch_shapes=[
            cols(BF16), cols(F32), heads(BF16, seq_len, chunk), cols(BF16), cols(BF16),
            heads(F32, num_blocks, dim), heads(BF16, chunk, dim), heads(F32, 8, dim),
            heads(F32, num_blocks, 2 * dim, dim), heads(BF16, num_blocks, chunk, 2 * dim),
            heads(F32, 2 * dim, dim), cols(BF16), cols(F32),
            heads(BF16, dim, dim), heads(F32, dim, dim),
            heads(BF16, dim, dim), heads(BF16, dim, dim), heads(BF16, dim, dim),
            pltpu.VMEM((num_heads // 2, dim, dim), BF16),
            pltpu.VMEM((num_forks, num_heads, dim, dim), BF16),
            pltpu.VMEM((num_blocks, HALO + chunk, width), BF16),
            pltpu.VMEM((3, width, head_cols), BF16),
            pltpu.VMEM((width, gate_down.shape[1]), BF16),
            pltpu.VMEM((3, HALO + chunk, span), F32),
            pltpu.VMEM((chunk, gate_down.shape[1]), BF16),
            pltpu.VMEM((chunk, num_heads), F32),
            pltpu.SemaphoreType.DMA((4,)),
            pltpu.SemaphoreType.DMA,
            pltpu.SemaphoreType.DMA,
            pltpu.SemaphoreType.DMA,
            pltpu.SemaphoreType.DMA((num_blocks,)),
            pltpu.SemaphoreType.DMA((num_blocks,)),
            pltpu.SemaphoreType.DMA((num_blocks,)),
            pltpu.SemaphoreType.DMA((num_heads // min(4, num_heads),)),
            pltpu.SemaphoreType.DMA((num_heads // min(4, num_heads),)),
            pltpu.SemaphoreType.DMA,
            pltpu.SemaphoreType.DMA,
            pltpu.SemaphoreType.DMA((num_ctx,)),
            pltpu.SemaphoreType.DMA((num_ctx,)),
        ],
        compiler_params=pltpu.CompilerParams(
            collective_id=0, has_side_effects=True, vmem_limit_bytes=60 << 20
        ),
        name="local",
    )(activations, w_query, w_key, w_value, conv_weight, gate_down, gate_up, w_beta, decay_rate, pos)


def solution(mesh):
    return jax.shard_map(
        per_device,
        mesh=mesh,
        in_specs=(
            P(("group", "ctx", "head"), None),
            P(None, "head"),
            P(None, "head"),
            P(None, "head"),
            P(None, None, "head"),
            P(),
            P(None, "head"),
            P(None, "head"),
            P("head"),
            P("group"),
        ),
        out_specs=(P(("group", "ctx"), "head"), P("group", "head", None, None)),
        check_vma=False,
    )
```

```python
import functools
import math

import jax
import jax.numpy as jnp
from jax import lax
from jax.experimental import pallas as pl
from jax.experimental.pallas import tpu as pltpu
from jax.sharding import PartitionSpec as P

HALO = 16
MESH = pl.DeviceIdType.MESH
F32 = jnp.float32
BF16 = jnp.bfloat16
NT = (((1,), (1,)), ((), ()))
TN = (((0,), (0,)), ((), ()))


def dot(left, right, dims=None):
    left, right = left.astype(BF16), right.astype(BF16)
    if dims is None:
        return jnp.dot(left, right, preferred_element_type=F32)
    return lax.dot_general(left, right, dims, preferred_element_type=F32)


def diagonal(one, two):
    top = jnp.concatenate([one, jnp.zeros(one.shape[:1] + two.shape[1:], BF16)], axis=1)
    low = jnp.concatenate([jnp.zeros(two.shape[:1] + one.shape[1:], BF16), two], axis=1)
    return jnp.concatenate([top, low], axis=0)


def twin_dots(left, right, dims=None):
    out = []
    for h in range(0, len(left), 2):
        wide = jnp.concatenate([left[h].astype(BF16), left[h + 1].astype(BF16)], axis=1)
        both = dot(wide, diagonal(right[h].astype(BF16), right[h + 1].astype(BF16)), dims)
        middle = both.shape[1] // 2
        out += [both[:, :middle], both[:, middle:]]
    return out


def softplus(value):
    return jnp.maximum(value, 0.0) + jnp.log1p(jnp.exp(-jnp.abs(value)))


def level_masks(chunk):
    row = lax.broadcasted_iota(jnp.int32, (chunk, chunk), 0)
    col = lax.broadcasted_iota(jnp.int32, (chunk, chunk), 1)
    masks = {}
    size = 1
    while size < chunk:
        differ = row ^ col
        masks[size] = (row > col) & (differ >= size) & (differ < 2 * size)
        size *= 2
    return row, col, masks


def level_reference(cum, size):
    chunk = cum.shape[0]
    if size >= 8:
        parts = cum.reshape(chunk // (2 * size), 2 * size, cum.shape[1])
        ref = parts[:, size - 1 : size, :]
        return jnp.broadcast_to(ref, parts.shape).reshape(cum.shape)
    parts = cum.reshape(chunk // 8, 8, cum.shape[1])
    place = lax.broadcasted_iota(jnp.int32, parts.shape, 1)
    ref = jnp.broadcast_to(parts[:, size - 1 : size, :], parts.shape)
    for start in range(2 * size, 8, 2 * size):
        ref = jnp.where(place >= start, parts[:, start + size - 1 : start + size, :], ref)
    return ref.reshape(cum.shape)


def copies_done(copies):
    for copy in copies:
        copy.wait()


def local_kernel(
    num_ctx, num_blocks,
    act_ref, wq_hbm, wk_hbm, wv_hbm, conv_ref, down_hbm, gu_ref, wb_ref, rate_ref, pos_ref,
    out_ref, forks_ref,
    w_ref, u_ref, qk_ref, qup_ref, kend_ref, dec_ref, kf_ref, df_ref,
    prefix_ref, change_ref, dev_ref, gain_ref, base_ref, fork_gain, fork_base,
    start_ref, end_ref, part_ref, other_ref, fork_ref,
    buf, weights, down_ref, ext_ref, latent_ref, beta_ref,
    load_sem, own_sem, halo_send, halo_recv, right_sem, left_sem, recv_sem,
    chain_send, chain_recv, pair_send, pair_recv, fork_send, fork_recv,
):
    chunk, width = act_ref.shape
    num_heads = rate_ref.shape[0]
    dim = gu_ref.shape[1] // num_heads
    group = min(4, num_heads)
    span = group * dim
    taps = conv_ref.shape[1]
    ctx, place = lax.axis_index("ctx"), lax.axis_index("head")
    rank = ctx * num_blocks + place
    position = pos_ref[ctx // 2] - ctx * (num_blocks * chunk)
    ranks = num_ctx * num_blocks
    after, before = (rank + 1) % ranks, (rank + ranks - 1) % ranks
    next_id = {"ctx": after // num_blocks, "head": after % num_blocks}
    prev_id = {"ctx": before // num_blocks, "head": before % num_blocks}

    loads = [
        pltpu.make_async_copy(src, weights.at[j], load_sem.at[j])
        for j, src in enumerate((wq_hbm, wk_hbm, wv_hbm))
    ] + [pltpu.make_async_copy(down_hbm, down_ref, load_sem.at[3])]
    own = pltpu.make_async_copy(act_ref, buf.at[place, pl.ds(HALO, chunk)], own_sem)
    own.start()
    for copy in loads:
        copy.start()
    barrier = pltpu.get_barrier_semaphore()
    for other in (next_id, prev_id):
        pl.semaphore_signal(barrier, inc=1, device_id=other, device_id_type=MESH)
    for turn in range(1, num_ctx):
        pl.semaphore_signal(
            barrier, inc=1, device_id={"ctx": (ctx + turn) % num_ctx}, device_id_type=MESH
        )
    pl.semaphore_wait(barrier, num_ctx + 1)
    halo = pltpu.make_async_remote_copy(
        src_ref=act_ref.at[pl.ds(chunk - HALO, HALO)],
        dst_ref=buf.at[after % num_blocks, pl.ds(0, HALO)],
        send_sem=halo_send, recv_sem=halo_recv, device_id=next_id, device_id_type=MESH,
    )
    halo.start()
    kf_ref[...] = jnp.zeros(kf_ref.shape, kf_ref.dtype)
    df_ref[...] = jnp.zeros(df_ref.shape, df_ref.dtype)
    own.wait()
    halo.wait()

    def to_right(i):
        block = jnp.maximum(place - i, 0)
        return pltpu.make_async_remote_copy(
            src_ref=buf.at[block], dst_ref=buf.at[block],
            send_sem=right_sem.at[i], recv_sem=recv_sem.at[block],
            device_id=next_id, device_id_type=MESH,
        )

    def to_left(i):
        block = jnp.minimum(place + i, num_blocks - 1)
        return pltpu.make_async_remote_copy(
            src_ref=buf.at[block], dst_ref=buf.at[block],
            send_sem=left_sem.at[i], recv_sem=recv_sem.at[block],
            device_id=prev_id, device_id_type=MESH,
        )

    def goes_right(i):
        return (place - i >= 0) & (place < num_blocks - 1) & (i < num_blocks - 1)

    def goes_left(i):
        return (place + i < num_blocks) & (place > 0) & (i < num_blocks - 1)

    row, col, masks = level_masks(chunk)
    eye = (row == col).astype(F32)
    tril = (row >= col).astype(BF16)
    heads = range(group)
    cut = lambda value, h: value[:, h * dim : (h + 1) * dim]

    def step(i, carry):
        @pl.when((i > 0) & (place - i >= 0))
        def _():
            to_right(i).wait_recv()

        @pl.when((i > 0) & (place + i < num_blocks))
        def _():
            to_left(i).wait_recv()

        @pl.when(goes_right(i))
        def _():
            to_right(i).start()

        @pl.when(goes_left(i))
        def _():
            to_left(i).start()

        @pl.when(i == 0)
        def _():
            copies_done(loads)

        over = (place + i) // num_blocks
        block = (place + i) * (1 - over) + (num_blocks - 1 - i) * over
        first_row = pl.multiple_of(block * chunk, chunk)
        rows = pl.ds(first_row, chunk)
        own_rows = buf[block, HALO:, :]
        latent_ref[...] = jnp.dot(own_rows, down_ref[...], preferred_element_type=F32).astype(BF16)
        beta_ref[...] = dot(own_rows, wb_ref[...], NT)
        halo_keep = jnp.where(ctx * num_blocks + block == 0, 0.0, 1.0).astype(F32)
        inner = position - block * chunk
        here = (inner >= 0) & (inner < chunk)

        def head_group(hg, carry):
            cols = pl.ds(pl.multiple_of(hg * span, span), span)
            acts = []
            for j in range(3):
                proj = jnp.dot(buf[block], weights[j, :, cols], preferred_element_type=F32)
                proj = proj.astype(BF16).astype(F32)
                ext_ref[j, 0:HALO, :] = proj[:HALO] * halo_keep
                ext_ref[j, HALO:, :] = proj[HALO:]
                start = HALO + 1 - taps
                mixed = sum(
                    conv_ref[j, tap : tap + 1, cols] * ext_ref[j, start + tap : start + tap + chunk, :]
                    for tap in range(taps)
                )
                acts.append(mixed / (1.0 + jnp.exp(-mixed)))

            def normed(value, factor):
                parts = []
                for h in heads:
                    part = cut(value, h)
                    total = jnp.sum(part * part, axis=-1, keepdims=True)
                    parts.append(part * (lax.rsqrt(total + 1e-06) * factor))
                return jnp.concatenate(parts, axis=1)

            query, key, value = normed(acts[0], 1.0 / math.sqrt(dim)), normed(acts[1], 1.0), acts[2]
            gate = softplus(jnp.dot(latent_ref[...], gu_ref[:, cols], preferred_element_type=F32))
            g = jnp.concatenate([cut(gate, h) * -rate_ref[hg * group + h] for h in heads], axis=1)
            lane = lax.broadcasted_iota(jnp.int32, beta_ref.shape, 1)
            betas = []
            for h in heads:
                pre = jnp.sum(jnp.where(lane == hg * group + h, beta_ref[...], 0.0), axis=1, keepdims=True)
                betas.append(1.0 / (1.0 + jnp.exp(-pre)))
            high = g.astype(BF16)
            low = (g - high.astype(F32)).astype(BF16)
            both = jnp.dot(tril, jnp.concatenate([high, low], axis=1), preferred_element_type=F32)
            cum = both[:, :span] + both[:, span:]
            product = query.astype(BF16).astype(F32) * key.astype(BF16).astype(F32)
            pair_k = [jnp.zeros((chunk, chunk), F32) for h in heads]
            pair_q = [
                jnp.where(row == col, jnp.sum(cut(product, h), axis=1, keepdims=True), 0.0) for h in heads
            ]
            for size, mask in masks.items():
                scale = jnp.exp(-jnp.abs(cum - level_reference(cum, size)))
                ks = (key * scale).astype(BF16)
                qs = (query * scale).astype(BF16)
                both = jnp.concatenate([ks, qs], axis=0)
                pairs = twin_dots([cut(both, h) for h in heads], [cut(ks, h) for h in heads], NT)
                pair_k = [jnp.where(mask, p[:chunk], old) for p, old in zip(pairs, pair_k)]
                pair_q = [jnp.where(mask, p[chunk:], old) for p, old in zip(pairs, pair_q)]
            system = [betas[h] * pair_k[h] for h in heads]
            inverse = [eye - jnp.where(masks[1], system[h], 0.0) for h in heads]
            for size, mask in masks.items():
                if size > 1:
                    left = twin_dots(inverse, [jnp.where(mask, system[h], 0.0) for h in heads])
                    right = twin_dots(left, inverse)
                    inverse = [inverse[h] - right[h] for h in heads]
            grown = jnp.exp(cum)
            key_up = key * grown
            last = cum[chunk - 1 : chunk, :]
            solved = [
                dot(inverse[h], jnp.concatenate([betas[h] * cut(value, h), betas[h] * cut(key_up, h)], axis=1))
                for h in heads
            ]
            u_ref[rows, cols] = jnp.concatenate([s[:, :dim] for s in solved], axis=1)
            w_ref[rows, cols] = jnp.concatenate([s[:, dim:] for s in solved], axis=1).astype(BF16)
            for h in heads:
                qk_ref[hg * group + h, rows, :] = pair_q[h].astype(BF16)
            qup_ref[rows, cols] = (query * grown).astype(BF16)
            kend_ref[rows, cols] = (key * jnp.exp(last - cum)).astype(BF16)
            whole = jnp.exp(last)
            at = jnp.sum(jnp.where(row[:, :1] == inner, cum, 0.0), axis=0, keepdims=True)
            keep = (row[:, :1] <= inner) & here
            kf_new = jnp.where(keep, key * jnp.exp(jnp.minimum(at - cum, 0.0)), 0.0)
            df_new = jnp.where(here, jnp.exp(at), 0.0)
            for h in heads:
                dec_ref[hg * group + h, pl.ds(block, 1), :] = cut(whole, h)
                kf_ref[hg * group + h] += cut(kf_new, h).astype(BF16)
                df_ref[hg * group + h] += jnp.broadcast_to(cut(df_new, h), (8, dim))
            return carry

        return lax.fori_loop(0, num_heads // group, head_group, carry)

    lax.fori_loop(0, num_blocks, step, 0)

    def compose(hg, carry):
        stacked = [jnp.concatenate([jnp.eye(dim, dtype=F32), jnp.zeros((dim, dim), F32)], axis=0) for h in heads]
        for c in range(num_blocks):
            rows = slice(c * chunk, (c + 1) * chunk)
            head_cols = [pl.ds(pl.multiple_of((hg * group + h) * dim, dim), dim) for h in heads]
            change = [
                (
                    jnp.concatenate([jnp.zeros((chunk, dim), F32), u_ref[rows, head_cols[h]]], axis=1)
                    - dot(w_ref[rows, head_cols[h]], stacked[h], NT)
                ).astype(BF16)
                for h in heads
            ]
            for h in heads:
                prefix_ref[hg * group + h, c] = stacked[h]
                change_ref[hg * group + h, c] = change[h]
            stacked = [
                stacked[h] * dec_ref[hg * group + h, c : c + 1, :]
                + dot(change[h], kend_ref[rows, head_cols[h]], TN)
                for h in heads
            ]
        for h in heads:
            dev_ref[hg * group + h] = stacked[h]
        return carry

    groups = num_heads // group
    lax.fori_loop(0, groups, compose, 0)

    @pl.when(ctx == 0)
    def _():
        start_ref[...] = jnp.zeros(start_ref.shape, BF16)

    def pass_on(gi):
        part = pl.ds(gi * group, group)
        return pltpu.make_async_remote_copy(
            src_ref=end_ref.at[part], dst_ref=start_ref.at[part],
            send_sem=chain_send.at[gi], recv_sem=chain_recv.at[gi],
            device_id={"ctx": jnp.minimum(ctx + 1, num_ctx - 1)}, device_id_type=MESH,
        )

    def chain():
        def one(gi, carry):
            @pl.when(ctx > 0)
            def _():
                pass_on(gi).wait_recv()

            @pl.when(ctx < num_ctx - 1)
            def _():
                ends = []
                for h in heads:
                    trans = dev_ref[gi * group + h, :dim, :]
                    fine = (trans - trans.astype(BF16).astype(F32)).astype(BF16)
                    first = start_ref[gi * group + h]
                    ends.append(dot(first, trans) + dot(first, fine) + dev_ref[gi * group + h, dim:, :])
                for h in heads:
                    end_ref[gi * group + h] = ends[h].astype(BF16)
                pass_on(gi).start()

            return carry

        lax.fori_loop(0, groups, one, 0)

    pair = 2
    which = jnp.clip(position, 0, num_blocks * chunk - 1) // chunk
    owned = (position >= 0) & (position < num_blocks * chunk)

    def read(j, carry):
        @pl.when(ctx == j)
        def _():
            chain()

        for p in range(pair):
            h = j * pair + p
            cols = pl.ds(pl.multiple_of(h * dim, dim), dim)
            for c in range(num_blocks):
                rows = slice(c * chunk, (c + 1) * chunk)
                both = dot(qup_ref[rows, cols], prefix_ref[h, c], NT) + dot(qk_ref[h, rows, :], change_ref[h, c])
                gain_ref[rows, cols] = both[:, :dim].astype(BF16)
                base_ref[rows, cols] = both[:, dim:]
            saved = prefix_ref[h, which] * df_ref[h, 0:1, :] + dot(change_ref[h, which], kf_ref[h], TN)
            fork_gain[h] = saved[:dim].T.astype(BF16)
            fork_base[h] = saved[dim:].T
        return carry

    parts = num_heads // pair
    lax.fori_loop(0, parts, read, 0)

    @pl.when(ctx >= parts)
    def _():
        chain()

    half = num_heads // 2
    core = ctx % 2
    mine = ctx // 2

    for h in range(num_heads):
        state = fork_base[h] + dot(fork_gain[h], start_ref[h], NT)
        part_ref[h] = jnp.where(owned, state, 0.0).astype(BF16)
    swap = pltpu.make_async_remote_copy(
        src_ref=part_ref.at[pl.ds((1 - core) * half, half)], dst_ref=other_ref,
        send_sem=pair_send, recv_sem=pair_recv,
        device_id={"ctx": mine * 2 + 1 - core}, device_id_type=MESH,
    )
    swap.start()

    def finish(h, carry):
        cols = pl.ds(pl.multiple_of(h * dim, dim), dim)
        out_ref[:, cols] = (base_ref[:, cols] + dot(gain_ref[:, cols], start_ref[h], NT)).astype(BF16)
        return carry

    lax.fori_loop(0, half, finish, 0)
    swap.wait()
    own_half = pl.ds(core * half, half)
    fork_ref[mine, own_half] = (part_ref[own_half].astype(F32) + other_ref[...].astype(F32)).astype(BF16)

    def share(turn, source):
        block = fork_ref.at[source // 2, pl.ds((source % 2) * half, half)]
        return pltpu.make_async_remote_copy(
            src_ref=block, dst_ref=block,
            send_sem=fork_send.at[turn], recv_sem=fork_recv.at[source],
            device_id={"ctx": (ctx + turn) % num_ctx}, device_id_type=MESH,
        )

    for turn in range(1, num_ctx):
        share(turn, ctx).start()
    lax.fori_loop(half, num_heads, finish, 0)
    for turn in range(1, num_ctx):
        share(turn, (ctx + turn) % num_ctx).wait_recv()
    for turn in range(1, num_ctx):
        share(turn, ctx).wait_send()
    forks_ref[...] = fork_ref[...]

    @pl.when(ctx < num_ctx - 1)
    def _():
        lax.fori_loop(0, groups, lambda gi, carry: (pass_on(gi).wait_send(), carry)[1], 0)

    def drain(i, carry):
        @pl.when(goes_right(i))
        def _():
            to_right(i).wait_send()

        @pl.when(goes_left(i))
        def _():
            to_left(i).wait_send()

        return carry

    lax.fori_loop(0, num_blocks - 1, drain, 0)


def per_device(
    activations, w_query, w_key, w_value, conv_weight, gate_down, gate_up, w_beta, decay_rate, fork_pos
):
    chunk, width = activations.shape
    num_blocks = lax.axis_size("head")
    seq_len = chunk * num_blocks
    num_heads = w_beta.shape[1]
    head_cols = w_query.shape[1]
    dim = head_cols // num_heads
    num_ctx = lax.axis_size("ctx")
    num_forks = fork_pos.shape[0]
    per_fork = num_ctx // num_forks
    assert per_fork == 2 and num_heads % 2 == 0
    span = min(4, num_heads) * dim

    smem = pl.BlockSpec(memory_space=pltpu.SMEM)
    vmem = pl.BlockSpec(memory_space=pltpu.VMEM)
    hbm = pl.BlockSpec(memory_space=pl.ANY)
    cols = lambda dtype: pltpu.VMEM((seq_len, head_cols), dtype)
    heads = lambda dtype, *shape: pltpu.VMEM((num_heads,) + shape, dtype)
    attended, forks = pl.pallas_call(
        functools.partial(local_kernel, num_ctx, num_blocks),
        in_specs=[vmem, hbm, hbm, hbm, vmem, hbm, vmem, vmem, smem, smem],
        out_specs=[vmem] * 2,
        out_shape=[
            jax.ShapeDtypeStruct((seq_len, head_cols), BF16),
            jax.ShapeDtypeStruct((num_forks, num_heads, dim, dim), BF16),
        ],
        scratch_shapes=[
            cols(BF16), cols(F32), heads(BF16, seq_len, chunk), cols(BF16), cols(BF16),
            heads(F32, num_blocks, dim), heads(BF16, chunk, dim), heads(F32, 8, dim),
            heads(F32, num_blocks, 2 * dim, dim), heads(BF16, num_blocks, chunk, 2 * dim),
            heads(F32, 2 * dim, dim), cols(BF16), cols(F32),
            heads(BF16, dim, dim), heads(F32, dim, dim),
            heads(BF16, dim, dim), heads(BF16, dim, dim), heads(BF16, dim, dim),
            pltpu.VMEM((num_heads // 2, dim, dim), BF16),
            pltpu.VMEM((num_forks, num_heads, dim, dim), BF16),
            pltpu.VMEM((num_blocks, HALO + chunk, width), BF16),
            pltpu.VMEM((3, width, head_cols), BF16),
            pltpu.VMEM((width, gate_down.shape[1]), BF16),
            pltpu.VMEM((3, HALO + chunk, span), F32),
            pltpu.VMEM((chunk, gate_down.shape[1]), BF16),
            pltpu.VMEM((chunk, num_heads), F32),
            pltpu.SemaphoreType.DMA((4,)),
            pltpu.SemaphoreType.DMA,
            pltpu.SemaphoreType.DMA,
            pltpu.SemaphoreType.DMA,
            pltpu.SemaphoreType.DMA((num_blocks,)),
            pltpu.SemaphoreType.DMA((num_blocks,)),
            pltpu.SemaphoreType.DMA((num_blocks,)),
            pltpu.SemaphoreType.DMA((num_heads // min(4, num_heads),)),
            pltpu.SemaphoreType.DMA((num_heads // min(4, num_heads),)),
            pltpu.SemaphoreType.DMA,
            pltpu.SemaphoreType.DMA,
            pltpu.SemaphoreType.DMA((num_ctx,)),
            pltpu.SemaphoreType.DMA((num_ctx,)),
        ],
        compiler_params=pltpu.CompilerParams(
            collective_id=0, has_side_effects=True, vmem_limit_bytes=60 << 20
        ),
        name="local",
    )(activations, w_query, w_key, w_value, conv_weight.transpose(1, 0, 2), gate_down, gate_up, w_beta.T, decay_rate, fork_pos)
    return attended, forks.astype(F32)


def solution(mesh):
    return jax.shard_map(
        per_device,
        mesh=mesh,
        in_specs=(
            P(("group", "ctx", "head"), None),
            P(None, "head"),
            P(None, "head"),
            P(None, "head"),
            P(None, None, "head"),
            P(),
            P(None, "head"),
            P(None, "head"),
            P("head"),
            P("group"),
        ),
        out_specs=(P(("group", "ctx"), "head"), P("group", "head", None, None)),
        check_vma=False,
    )
```

```python
import functools
import math

import jax
import jax.numpy as jnp
from jax import lax
from jax.experimental import pallas as pl
from jax.experimental.pallas import tpu as pltpu
from jax.sharding import PartitionSpec as P

HALO = 8
MESH = pl.DeviceIdType.MESH
F32 = jnp.float32
BF16 = jnp.bfloat16
NT = (((1,), (1,)), ((), ()))
TN = (((0,), (0,)), ((), ()))


def dot(left, right, dims=None):
    left, right = left.astype(BF16), right.astype(BF16)
    if dims is None:
        return jnp.dot(left, right, preferred_element_type=F32)
    return lax.dot_general(left, right, dims, preferred_element_type=F32)


def diagonal(one, two):
    top = jnp.concatenate([one, jnp.zeros(one.shape[:1] + two.shape[1:], BF16)], axis=1)
    low = jnp.concatenate([jnp.zeros(two.shape[:1] + one.shape[1:], BF16), two], axis=1)
    return jnp.concatenate([top, low], axis=0)


def twin_dots(left, right, dims=None):
    out = []
    for h in range(0, len(left), 2):
        wide = jnp.concatenate([left[h].astype(BF16), left[h + 1].astype(BF16)], axis=1)
        both = dot(wide, diagonal(right[h].astype(BF16), right[h + 1].astype(BF16)), dims)
        middle = both.shape[1] // 2
        out += [both[:, :middle], both[:, middle:]]
    return out


def softplus(value):
    return jnp.maximum(value, 0.0) + jnp.log1p(jnp.exp(-jnp.abs(value)))


def level_masks(chunk):
    row = lax.broadcasted_iota(jnp.int32, (chunk, chunk), 0)
    col = lax.broadcasted_iota(jnp.int32, (chunk, chunk), 1)
    masks = {}
    size = 1
    while size < chunk:
        differ = row ^ col
        masks[size] = (row > col) & (differ >= size) & (differ < 2 * size)
        size *= 2
    return row, col, masks


def level_reference(cum, size):
    chunk = cum.shape[0]
    if size >= 8:
        parts = cum.reshape(chunk // (2 * size), 2 * size, cum.shape[1])
        ref = parts[:, size - 1 : size, :]
        return jnp.broadcast_to(ref, parts.shape).reshape(cum.shape)
    parts = cum.reshape(chunk // 8, 8, cum.shape[1])
    place = lax.broadcasted_iota(jnp.int32, parts.shape, 1)
    ref = jnp.broadcast_to(parts[:, size - 1 : size, :], parts.shape)
    for start in range(2 * size, 8, 2 * size):
        ref = jnp.where(place >= start, parts[:, start + size - 1 : start + size, :], ref)
    return ref.reshape(cum.shape)


def copies_done(copies):
    for copy in copies:
        copy.wait()


def local_kernel(
    num_ctx, num_blocks,
    act_ref, wq_hbm, wk_hbm, wv_hbm, conv_ref, down_hbm, gu_ref, wb_ref, rate_ref, pos_ref,
    out_ref, forks_ref,
    w_ref, u_ref, qk_ref, qup_ref, kend_ref, dec_ref, kf_ref, df_ref,
    prefix_ref, change_ref, dev_ref, gain_ref, base_ref, fork_gain, fork_base,
    start_ref, end_ref, part_ref, other_ref, fork_ref,
    buf, weights, down_ref, ext_ref, latent_ref, beta_ref,
    load_sem, own_sem, halo_send, halo_recv, right_sem, left_sem, recv_sem,
    chain_send, chain_recv, pair_send, pair_recv, fork_send, fork_recv,
):
    chunk, width = act_ref.shape
    num_heads = rate_ref.shape[0]
    dim = gu_ref.shape[1] // num_heads
    group = min(4, num_heads)
    span = group * dim
    taps = conv_ref.shape[1]
    ctx, place = lax.axis_index("ctx"), lax.axis_index("head")
    rank = ctx * num_blocks + place
    position = pos_ref[ctx // 2] - ctx * (num_blocks * chunk)
    ranks = num_ctx * num_blocks
    after, before = (rank + 1) % ranks, (rank + ranks - 1) % ranks
    next_id = {"ctx": after // num_blocks, "head": after % num_blocks}
    prev_id = {"ctx": before // num_blocks, "head": before % num_blocks}

    loads = [
        pltpu.make_async_copy(src, weights.at[j], load_sem.at[j])
        for j, src in enumerate((wq_hbm, wk_hbm, wv_hbm))
    ] + [pltpu.make_async_copy(down_hbm, down_ref, load_sem.at[3])]
    own = pltpu.make_async_copy(act_ref, buf.at[place, pl.ds(HALO, chunk)], own_sem)
    own.start()
    for copy in loads:
        copy.start()
    barrier = pltpu.get_barrier_semaphore()
    for other in (next_id, prev_id):
        pl.semaphore_signal(barrier, inc=1, device_id=other, device_id_type=MESH)
    for turn in range(1, num_ctx):
        pl.semaphore_signal(
            barrier, inc=1, device_id={"ctx": (ctx + turn) % num_ctx}, device_id_type=MESH
        )
    pl.semaphore_wait(barrier, num_ctx + 1)
    halo = pltpu.make_async_remote_copy(
        src_ref=act_ref.at[pl.ds(chunk - HALO, HALO)],
        dst_ref=buf.at[after % num_blocks, pl.ds(0, HALO)],
        send_sem=halo_send, recv_sem=halo_recv, device_id=next_id, device_id_type=MESH,
    )
    halo.start()
    kf_ref[...] = jnp.zeros(kf_ref.shape, kf_ref.dtype)
    df_ref[...] = jnp.zeros(df_ref.shape, df_ref.dtype)
    own.wait()
    halo.wait()

    def to_right(i):
        block = jnp.maximum(place - i, 0)
        return pltpu.make_async_remote_copy(
            src_ref=buf.at[block], dst_ref=buf.at[block],
            send_sem=right_sem.at[i], recv_sem=recv_sem.at[block],
            device_id=next_id, device_id_type=MESH,
        )

    def to_left(i):
        block = jnp.minimum(place + i, num_blocks - 1)
        return pltpu.make_async_remote_copy(
            src_ref=buf.at[block], dst_ref=buf.at[block],
            send_sem=left_sem.at[i], recv_sem=recv_sem.at[block],
            device_id=prev_id, device_id_type=MESH,
        )

    def goes_right(i):
        return (place - i >= 0) & (place < num_blocks - 1) & (i < num_blocks - 1)

    def goes_left(i):
        return (place + i < num_blocks) & (place > 0) & (i < num_blocks - 1)

    row, col, masks = level_masks(chunk)
    eye = (row == col).astype(F32)
    tril = (row >= col).astype(BF16)
    heads = range(group)
    cut = lambda value, h: value[:, h * dim : (h + 1) * dim]

    def step(i, carry):
        @pl.when((i > 0) & (place - i >= 0))
        def _():
            to_right(i).wait_recv()

        @pl.when((i > 0) & (place + i < num_blocks))
        def _():
            to_left(i).wait_recv()

        @pl.when(goes_right(i))
        def _():
            to_right(i).start()

        @pl.when(goes_left(i))
        def _():
            to_left(i).start()

        @pl.when(i == 0)
        def _():
            copies_done(loads)

        over = (place + i) // num_blocks
        block = (place + i) * (1 - over) + (num_blocks - 1 - i) * over
        first_row = pl.multiple_of(block * chunk, chunk)
        rows = pl.ds(first_row, chunk)
        own_rows = buf[block, HALO:, :]
        latent_ref[...] = jnp.dot(own_rows, down_ref[...], preferred_element_type=F32).astype(BF16)
        beta_ref[...] = dot(own_rows, wb_ref[...], NT)
        halo_keep = jnp.where(ctx * num_blocks + block == 0, 0.0, 1.0).astype(F32)
        inner = position - block * chunk
        here = (inner >= 0) & (inner < chunk)

        def head_group(hg, carry):
            cols = pl.ds(pl.multiple_of(hg * span, span), span)
            acts = []
            for j in range(3):
                proj = jnp.dot(buf[block], weights[j, :, cols], preferred_element_type=F32)
                proj = proj.astype(BF16).astype(F32)
                ext_ref[j, 0:HALO, :] = proj[:HALO] * halo_keep
                ext_ref[j, HALO:, :] = proj[HALO:]
                start = HALO + 1 - taps
                mixed = sum(
                    conv_ref[j, tap : tap + 1, cols] * ext_ref[j, start + tap : start + tap + chunk, :]
                    for tap in range(taps)
                )
                acts.append(mixed / (1.0 + jnp.exp(-mixed)))

            def normed(value, factor):
                parts = []
                for h in heads:
                    part = cut(value, h)
                    total = jnp.sum(part * part, axis=-1, keepdims=True)
                    parts.append(part * (lax.rsqrt(total + 1e-06) * factor))
                return jnp.concatenate(parts, axis=1)

            query, key, value = normed(acts[0], 1.0 / math.sqrt(dim)), normed(acts[1], 1.0), acts[2]
            gate = softplus(jnp.dot(latent_ref[...], gu_ref[:, cols], preferred_element_type=F32))
            g = jnp.concatenate([cut(gate, h) * -rate_ref[hg * group + h] for h in heads], axis=1)
            lane = lax.broadcasted_iota(jnp.int32, beta_ref.shape, 1)
            betas = []
            for h in heads:
                pre = jnp.sum(jnp.where(lane == hg * group + h, beta_ref[...], 0.0), axis=1, keepdims=True)
                betas.append(1.0 / (1.0 + jnp.exp(-pre)))
            high = g.astype(BF16)
            low = (g - high.astype(F32)).astype(BF16)
            both = jnp.dot(tril, jnp.concatenate([high, low], axis=1), preferred_element_type=F32)
            cum = both[:, :span] + both[:, span:]
            product = query.astype(BF16).astype(F32) * key.astype(BF16).astype(F32)
            pair_k = [jnp.zeros((chunk, chunk), F32) for h in heads]
            pair_q = [
                jnp.where(row == col, jnp.sum(cut(product, h), axis=1, keepdims=True), 0.0) for h in heads
            ]
            for size, mask in masks.items():
                scale = jnp.exp(-jnp.abs(cum - level_reference(cum, size)))
                ks = (key * scale).astype(BF16)
                qs = (query * scale).astype(BF16)
                both = jnp.concatenate([ks, qs], axis=0)
                pairs = twin_dots([cut(both, h) for h in heads], [cut(ks, h) for h in heads], NT)
                pair_k = [jnp.where(mask, p[:chunk], old) for p, old in zip(pairs, pair_k)]
                pair_q = [jnp.where(mask, p[chunk:], old) for p, old in zip(pairs, pair_q)]
            system = [betas[h] * pair_k[h] for h in heads]
            inverse = [eye - jnp.where(masks[1], system[h], 0.0) for h in heads]
            for size, mask in masks.items():
                if size > 1:
                    left = twin_dots(inverse, [jnp.where(mask, system[h], 0.0) for h in heads])
                    right = twin_dots(left, inverse)
                    inverse = [inverse[h] - right[h] for h in heads]
            grown = jnp.exp(cum)
            key_up = key * grown
            last = cum[chunk - 1 : chunk, :]
            solved = [
                dot(inverse[h], jnp.concatenate([betas[h] * cut(value, h), betas[h] * cut(key_up, h)], axis=1))
                for h in heads
            ]
            u_ref[rows, cols] = jnp.concatenate([s[:, :dim] for s in solved], axis=1)
            w_ref[rows, cols] = jnp.concatenate([s[:, dim:] for s in solved], axis=1).astype(BF16)
            for h in heads:
                qk_ref[hg * group + h, rows, :] = pair_q[h].astype(BF16)
            qup_ref[rows, cols] = (query * grown).astype(BF16)
            kend_ref[rows, cols] = (key * jnp.exp(last - cum)).astype(BF16)
            whole = jnp.exp(last)
            at = jnp.sum(jnp.where(row[:, :1] == inner, cum, 0.0), axis=0, keepdims=True)
            keep = (row[:, :1] <= inner) & here
            kf_new = jnp.where(keep, key * jnp.exp(jnp.minimum(at - cum, 0.0)), 0.0)
            df_new = jnp.where(here, jnp.exp(at), 0.0)
            for h in heads:
                dec_ref[hg * group + h, pl.ds(block, 1), :] = cut(whole, h)
                kf_ref[hg * group + h] += cut(kf_new, h).astype(BF16)
                df_ref[hg * group + h] += jnp.broadcast_to(cut(df_new, h), (8, dim))
            return carry

        return lax.fori_loop(0, num_heads // group, head_group, carry)

    lax.fori_loop(0, num_blocks, step, 0)

    def compose(hg, carry):
        stacked = [jnp.concatenate([jnp.eye(dim, dtype=F32), jnp.zeros((dim, dim), F32)], axis=0) for h in heads]
        for c in range(num_blocks):
            rows = slice(c * chunk, (c + 1) * chunk)
            head_cols = [pl.ds(pl.multiple_of((hg * group + h) * dim, dim), dim) for h in heads]
            change = [
                (
                    jnp.concatenate([jnp.zeros((chunk, dim), F32), u_ref[rows, head_cols[h]]], axis=1)
                    - dot(w_ref[rows, head_cols[h]], stacked[h], NT)
                ).astype(BF16)
                for h in heads
            ]
            for h in heads:
                prefix_ref[hg * group + h, c] = stacked[h]
                change_ref[hg * group + h, c] = change[h]
            stacked = [
                stacked[h] * dec_ref[hg * group + h, c : c + 1, :]
                + dot(change[h], kend_ref[rows, head_cols[h]], TN)
                for h in heads
            ]
        for h in heads:
            dev_ref[hg * group + h] = stacked[h]
        return carry

    groups = num_heads // group
    lax.fori_loop(0, groups, compose, 0)

    @pl.when(ctx == 0)
    def _():
        start_ref[...] = jnp.zeros(start_ref.shape, BF16)

    def pass_on(gi):
        part = pl.ds(gi * group, group)
        return pltpu.make_async_remote_copy(
            src_ref=end_ref.at[part], dst_ref=start_ref.at[part],
            send_sem=chain_send.at[gi], recv_sem=chain_recv.at[gi],
            device_id={"ctx": jnp.minimum(ctx + 1, num_ctx - 1)}, device_id_type=MESH,
        )

    def chain():
        def one(gi, carry):
            @pl.when(ctx > 0)
            def _():
                pass_on(gi).wait_recv()

            @pl.when(ctx < num_ctx - 1)
            def _():
                ends = []
                for h in heads:
                    trans = dev_ref[gi * group + h, :dim, :]
                    fine = (trans - trans.astype(BF16).astype(F32)).astype(BF16)
                    first = start_ref[gi * group + h]
                    ends.append(dot(first, trans) + dot(first, fine) + dev_ref[gi * group + h, dim:, :])
                for h in heads:
                    end_ref[gi * group + h] = ends[h].astype(BF16)
                pass_on(gi).start()

            return carry

        lax.fori_loop(0, groups, one, 0)

    pair = 2
    which = jnp.clip(position, 0, num_blocks * chunk - 1) // chunk
    owned = (position >= 0) & (position < num_blocks * chunk)

    def read(j, carry):
        @pl.when(ctx == j)
        def _():
            chain()

        for p in range(pair):
            h = j * pair + p
            cols = pl.ds(pl.multiple_of(h * dim, dim), dim)
            for c in range(num_blocks):
                rows = slice(c * chunk, (c + 1) * chunk)
                both = dot(qup_ref[rows, cols], prefix_ref[h, c], NT) + dot(qk_ref[h, rows, :], change_ref[h, c])
                gain_ref[rows, cols] = both[:, :dim].astype(BF16)
                base_ref[rows, cols] = both[:, dim:]
            saved = prefix_ref[h, which] * df_ref[h, 0:1, :] + dot(change_ref[h, which], kf_ref[h], TN)
            fork_gain[h] = saved[:dim].T.astype(BF16)
            fork_base[h] = saved[dim:].T
        return carry

    parts = num_heads // pair
    lax.fori_loop(0, parts, read, 0)

    @pl.when(ctx >= parts)
    def _():
        chain()

    half = num_heads // 2
    core = ctx % 2
    mine = ctx // 2

    for h in range(num_heads):
        state = fork_base[h] + dot(fork_gain[h], start_ref[h], NT)
        part_ref[h] = jnp.where(owned, state, 0.0).astype(BF16)
    swap = pltpu.make_async_remote_copy(
        src_ref=part_ref.at[pl.ds((1 - core) * half, half)], dst_ref=other_ref,
        send_sem=pair_send, recv_sem=pair_recv,
        device_id={"ctx": mine * 2 + 1 - core}, device_id_type=MESH,
    )
    swap.start()

    def finish(h, carry):
        cols = pl.ds(pl.multiple_of(h * dim, dim), dim)
        out_ref[:, cols] = (base_ref[:, cols] + dot(gain_ref[:, cols], start_ref[h], NT)).astype(BF16)
        return carry

    lax.fori_loop(0, half, finish, 0)
    swap.wait()
    own_half = pl.ds(core * half, half)
    fork_ref[mine, own_half] = (part_ref[own_half].astype(F32) + other_ref[...].astype(F32)).astype(BF16)

    def share(turn, source):
        block = fork_ref.at[source // 2, pl.ds((source % 2) * half, half)]
        return pltpu.make_async_remote_copy(
            src_ref=block, dst_ref=block,
            send_sem=fork_send.at[turn], recv_sem=fork_recv.at[source],
            device_id={"ctx": (ctx + turn) % num_ctx}, device_id_type=MESH,
        )

    for turn in range(1, num_ctx):
        share(turn, ctx).start()
    lax.fori_loop(half, num_heads, finish, 0)
    for turn in range(1, num_ctx):
        share(turn, (ctx + turn) % num_ctx).wait_recv()
    for turn in range(1, num_ctx):
        share(turn, ctx).wait_send()
    forks_ref[...] = fork_ref[...]

    @pl.when(ctx < num_ctx - 1)
    def _():
        lax.fori_loop(0, groups, lambda gi, carry: (pass_on(gi).wait_send(), carry)[1], 0)

    def drain(i, carry):
        @pl.when(goes_right(i))
        def _():
            to_right(i).wait_send()

        @pl.when(goes_left(i))
        def _():
            to_left(i).wait_send()

        return carry

    lax.fori_loop(0, num_blocks - 1, drain, 0)


def per_device(
    activations, w_query, w_key, w_value, conv_weight, gate_down, gate_up, w_beta, decay_rate, fork_pos
):
    chunk, width = activations.shape
    num_blocks = lax.axis_size("head")
    seq_len = chunk * num_blocks
    num_heads = w_beta.shape[1]
    head_cols = w_query.shape[1]
    dim = head_cols // num_heads
    num_ctx = lax.axis_size("ctx")
    num_forks = fork_pos.shape[0]
    per_fork = num_ctx // num_forks
    assert per_fork == 2 and num_heads % 2 == 0
    span = min(4, num_heads) * dim

    smem = pl.BlockSpec(memory_space=pltpu.SMEM)
    vmem = pl.BlockSpec(memory_space=pltpu.VMEM)
    hbm = pl.BlockSpec(memory_space=pl.ANY)
    cols = lambda dtype: pltpu.VMEM((seq_len, head_cols), dtype)
    heads = lambda dtype, *shape: pltpu.VMEM((num_heads,) + shape, dtype)
    attended, forks = pl.pallas_call(
        functools.partial(local_kernel, num_ctx, num_blocks),
        in_specs=[vmem, hbm, hbm, hbm, vmem, hbm, vmem, vmem, smem, smem],
        out_specs=[vmem] * 2,
        out_shape=[
            jax.ShapeDtypeStruct((seq_len, head_cols), BF16),
            jax.ShapeDtypeStruct((num_forks, num_heads, dim, dim), BF16),
        ],
        scratch_shapes=[
            cols(BF16), cols(F32), heads(BF16, seq_len, chunk), cols(BF16), cols(BF16),
            heads(F32, num_blocks, dim), heads(BF16, chunk, dim), heads(F32, 8, dim),
            heads(F32, num_blocks, 2 * dim, dim), heads(BF16, num_blocks, chunk, 2 * dim),
            heads(F32, 2 * dim, dim), cols(BF16), cols(F32),
            heads(BF16, dim, dim), heads(F32, dim, dim),
            heads(BF16, dim, dim), heads(BF16, dim, dim), heads(BF16, dim, dim),
            pltpu.VMEM((num_heads // 2, dim, dim), BF16),
            pltpu.VMEM((num_forks, num_heads, dim, dim), BF16),
            pltpu.VMEM((num_blocks, HALO + chunk, width), BF16),
            pltpu.VMEM((3, width, head_cols), BF16),
            pltpu.VMEM((width, gate_down.shape[1]), BF16),
            pltpu.VMEM((3, HALO + chunk, span), F32),
            pltpu.VMEM((chunk, gate_down.shape[1]), BF16),
            pltpu.VMEM((chunk, num_heads), F32),
            pltpu.SemaphoreType.DMA((4,)),
            pltpu.SemaphoreType.DMA,
            pltpu.SemaphoreType.DMA,
            pltpu.SemaphoreType.DMA,
            pltpu.SemaphoreType.DMA((num_blocks,)),
            pltpu.SemaphoreType.DMA((num_blocks,)),
            pltpu.SemaphoreType.DMA((num_blocks,)),
            pltpu.SemaphoreType.DMA((num_heads // min(4, num_heads),)),
            pltpu.SemaphoreType.DMA((num_heads // min(4, num_heads),)),
            pltpu.SemaphoreType.DMA,
            pltpu.SemaphoreType.DMA,
            pltpu.SemaphoreType.DMA((num_ctx,)),
            pltpu.SemaphoreType.DMA((num_ctx,)),
        ],
        compiler_params=pltpu.CompilerParams(
            collective_id=0, has_side_effects=True, vmem_limit_bytes=60 << 20
        ),
        name="local",
    )(activations, w_query, w_key, w_value, conv_weight.transpose(1, 0, 2), gate_down, gate_up, w_beta.T, decay_rate, fork_pos)
    return attended, forks.astype(F32)


def solution(mesh):
    return jax.shard_map(
        per_device,
        mesh=mesh,
        in_specs=(
            P(("group", "ctx", "head"), None),
            P(None, "head"),
            P(None, "head"),
            P(None, "head"),
            P(None, None, "head"),
            P(),
            P(None, "head"),
            P(None, "head"),
            P("head"),
            P("group"),
        ),
        out_specs=(P(("group", "ctx"), "head"), P("group", "head", None, None)),
        check_vma=False,
    )
```
